512 devices in a mesh: dp: 32 (over z, y_lo), fsdp: 16 (over x, y_hi, core).
Axes of the slice: x: 4, y: 4 (y_hi: 2, y_lo: 2; y = y_hi * 2 + y_lo), z: 16, core: 2. Of those that a mesh axis runs over, the one named last changes fastest.
Arguments:
- tokens: bfloat16 [65536, 1024], P(('dp', 'fsdp')), may hold values from -6 to 6
- cotangent: bfloat16 [65536, 1024], P(('dp', 'fsdp')), may hold values from -6 to 6
- routes: int32 [65536, 1], P(('dp', 'fsdp')), may hold values from 0 to 32; in each aligned block of 128 rows (0 to 127, 128 to 255, ...) at most 4 rows name the same one
- norm_gain_vector: float32 [1024], replicated, may hold values from 0.25 to 1.75
- up_weight: bfloat16 [1024, 4096], P(None, 'fsdp'), may hold values from -0.1875 to 0.1875
- up_bias: float32 [4096], P('fsdp'), may hold values from -4 to 4
- down_weight: bfloat16 [4096, 1024], P('fsdp'), may hold values from -0.09375 to 0.09375
Outputs:
- input_grad: bfloat16 [65536, 1024], P(('dp', 'fsdp'))
- up_grad: float32 [1024, 4096], P(None, 'fsdp')
- bias_grad: float32 [4096], P('fsdp')
- down_grad: float32 [4096, 1024], P('fsdp')
- gain_grad: float32 [1024], replicated
The draws below stay inside these ranges and needn't reach their ends.
Inputs may be any that keep to these rules, and one draw needn't show every extreme that they name: `routes`: among the 128 slots of one device no value below 32 appears more than 4 times; the value 32 marks a padding slot.
All inputs are finite; a program needn't handle non-finite values.
Results may differ from the reference program's by a relative error of at most 0.024.
Values may be sent and summed in bfloat16 or wider, within the bound.
A program may use at most 128 MiB of HBM per device.

```python
import math
import jax
import jax.numpy as jnp
import numpy as np
from jax import lax

D = 1024
FF = 4096
ROWS = 128
CAP = 4
TOKENS = 65536
N_DP = 32
N_FSDP = 16


def block_scale(rng, dims, split, least, largest):
    gain = 1.0
    for dim, parts in split:
        steps = jax.random.uniform(jax.random.fold_in(jax.random.fold_in(rng, 6), dim), (parts,), jnp.float32, least / len(split), largest / len(split))
        gain = gain * jnp.repeat(jnp.exp(steps), dims[dim] // parts).reshape((-1,) + (1,) * (len(dims) - 1 - dim))
    return gain


def deal_out(rng, own, number, rows, number_of, top, reach, lean):
    order = jax.random.permutation(rng, number_of)
    heavy_load, ordinary = load_shares(number_of, rows * top, reach, lean, True), load_shares(number_of, rows * top, reach, lean, False)
    places = jnp.arange(number_of)

    def named(lengths, rotation):
        used = int((lengths > 0).sum())
        fixed = max(1, used // 4)
        shifted = fixed + (places - fixed + rotation * (used - fixed)) % max(1, number_of - fixed)
        return jnp.zeros((number_of,), jnp.int32).at[order[jnp.where(places < fixed, places, shifted)]].set(jnp.asarray(lengths, jnp.int32))

    lengths = jnp.where(number % 4 == 0, named(heavy_load, number // 4), named(ordinary, number - number // 4 - 1))
    mixed = jax.random.permutation(jax.random.fold_in(own, 3), number_of)
    giver, receiver = mixed[0:number_of // 2 * 2:2], mixed[1:number_of // 2 * 2:2]
    room = jnp.minimum(lengths[giver] - 1, reach - lengths[receiver]) // 2
    room = jnp.where((giver == order[0]) | (receiver == order[0]) | (lengths[receiver] == 0), 0, jnp.maximum(room, 0))
    shifted = jax.random.randint(jax.random.fold_in(own, 4), (number_of // 2,), 0, 1 << 20) % (room + 1)
    lengths = lengths.at[giver].add(-shifted).at[receiver].add(shifted)
    items = jnp.searchsorted(jnp.cumsum(lengths), jnp.arange(rows * top), side="right").astype(jnp.int32)
    grid = items.reshape(top, rows).T
    grid = grid[jax.random.permutation(jax.random.fold_in(own, 1), rows)]
    rotation = jax.random.randint(jax.random.fold_in(own, 2), (rows, 1), 0, top)
    return jnp.take_along_axis(grid, (jnp.arange(top)[None, :] + rotation) % top, axis=1)


def load_shares(number_of, total, reach, skew, full):
    portions = [(1 << 20) // math.isqrt(standing ** skew) + 1 for standing in range(1, number_of + 1)]
    largest = reach if full else min(reach, max(-(-total // number_of), total * portions[0] // sum(portions)))
    least = 1 if total - largest >= number_of - 1 else 0
    holding, spare = [largest] + [least] * (number_of - 1), total - largest - least * (number_of - 1)
    while spare > 0:
        free = [i for i in range(1, number_of) if holding[i] < largest] or [i for i in range(1, number_of) if holding[i] < reach]
        mass, remaining = sum([portions[i] for i in free]), spare
        for i in free:
            extra = min(reach - holding[i], max(1, remaining * portions[i] // mass), spare)
            holding[i] = holding[i] + extra
            spare = spare - extra
    return np.array(holding)


def normal_values(rng, dims, scale, bound, cuts=(), held_as=jnp.bfloat16):
    array = scale * jax.random.normal(rng, dims, jnp.float32)
    if cuts:
        array = array * block_scale(rng, dims, cuts, -0.22, 0.18)
    return jnp.clip(array, -bound, bound).astype(held_as)


def setup_inputs(seed: int = 0) -> dict:
    streams_of = jax.random.split(jax.random.key(seed), 8)
    tokens = normal_values(streams_of[0], (TOKENS, D), 1.0, 6.0, ((0, 512),))
    cotangent = normal_values(streams_of[1], (TOKENS, D), 1.0, 6.0, ((0, 512),))
    routes_keys = jax.random.split(jax.random.fold_in(streams_of[2], 1), TOKENS // ROWS)
    routes_turns = jax.random.permutation(jax.random.fold_in(streams_of[2], 3), TOKENS // ROWS)
    routes = jax.vmap(lambda own, number: deal_out(jax.random.fold_in(streams_of[2], 2), own, number, ROWS, N_DP + 1, 1, CAP, 2))(routes_keys, routes_turns).reshape((TOKENS, 1))
    norm_gain_vector = jnp.clip(1.0 + 0.15 * jax.random.normal(streams_of[3], (D,), jnp.float32), 0.25, 1.75)
    up_weight = normal_values(streams_of[4], (D, FF), D ** -0.5, 0.1875, ((1, 16),))
    up_bias = normal_values(streams_of[5], (FF,), 1.0, 4.0, ((0, 16),), jnp.float32)
    down_weight = normal_values(streams_of[6], (FF, D), FF ** -0.5, 0.09375, ((0, 16),))
    return dict(tokens=tokens, cotangent=cotangent, routes=routes, norm_gain_vector=norm_gain_vector, up_weight=up_weight, up_bias=up_bias, down_weight=down_weight)


root_two_pi = 0.7978845608
cubic = 0.044715

def gelu_pair(pre):
    inner = root_two_pi * (pre + cubic * pre * pre * pre)
    tangent = jnp.tanh(inner)
    act = 0.5 * pre * (1.0 + tangent)
    slope = 0.5 * (1.0 + tangent) + 0.5 * pre * (1.0 - tangent * tangent) * root_two_pi * (1.0 + 3.0 * cubic * pre * pre)
    return (act, slope)

def apply_layer_norm(values):
    row_average = lax.optimization_barrier(jnp.mean(values, axis=1, keepdims=True))
    centered = values - row_average
    variance = lax.optimization_barrier(jnp.mean(centered * centered, axis=1, keepdims=True))
    inverse_std = 1.0 / jnp.sqrt(variance + 1e-05)
    return (centered * inverse_std, inverse_std)

def reference(tokens, cotangent, routes, norm_gain_vector, up_weight, up_bias, down_weight):
    capacity = ROWS // N_DP
    target = routes[:, 0].reshape(N_DP, N_FSDP, ROWS)
    matches = (target[..., None] == jnp.arange(N_DP + 1, dtype=jnp.int32)).astype(jnp.int32)
    earlier = jnp.cumsum(matches, axis=2) - matches
    ranked = lax.optimization_barrier(jnp.sum(earlier * matches, axis=3)).astype(jnp.int32)
    source = jnp.broadcast_to(jnp.arange(N_DP, dtype=jnp.int32)[:, None, None], target.shape)
    column = jnp.broadcast_to(jnp.arange(N_FSDP, dtype=jnp.int32)[None, :, None], target.shape)
    place = (source * capacity + ranked).astype(jnp.int32)
    inputs4 = tokens.reshape(N_DP, N_FSDP, ROWS, D)
    cot4 = cotangent.reshape(N_DP, N_FSDP, ROWS, D)
    packed_in = jnp.zeros((N_DP, N_FSDP, ROWS, D), jnp.bfloat16).at[target, column, place].set(inputs4, mode='drop')
    packed_cot = jnp.zeros((N_DP, N_FSDP, ROWS, D), jnp.bfloat16).at[target, column, place].set(cot4, mode='drop')
    block = FF // N_FSDP

    def group(pair):
        group_input_rows, group_cotangent_rows = pair
        group_input_rows = group_input_rows.reshape(N_FSDP * ROWS, D)
        group_cotangent_rows = group_cotangent_rows.reshape(N_FSDP * ROWS, D)
        standardized_rows, inverse_std = apply_layer_norm(group_input_rows.astype(jnp.float32))
        normed_values = (standardized_rows * norm_gain_vector).astype(jnp.bfloat16)
        pre = jnp.dot(normed_values, up_weight, preferred_element_type=jnp.float32) + up_bias
        act_full, slope = gelu_pair(pre)
        act = act_full.astype(jnp.bfloat16)
        act_grad = jnp.dot(group_cotangent_rows, down_weight.T, preferred_element_type=jnp.float32)
        pre_grad = (act_grad * slope).astype(jnp.bfloat16)
        down_part = jnp.dot(act.T, group_cotangent_rows, preferred_element_type=jnp.float32)
        up_part = jnp.dot(normed_values.T, pre_grad, preferred_element_type=jnp.float32)
        bias_part = lax.optimization_barrier(jnp.sum(pre_grad.astype(jnp.float32), axis=0))
        normed_rows_gradient = jnp.zeros((N_FSDP * ROWS, D), jnp.float32)
        for index in range(N_FSDP):
            partial_term = jnp.dot(pre_grad[:, index * block:(index + 1) * block], up_weight[:, index * block:(index + 1) * block].T, preferred_element_type=jnp.float32)
            rounded = lax.optimization_barrier(partial_term.astype(jnp.bfloat16))
            normed_rows_gradient = normed_rows_gradient + rounded.astype(jnp.float32)
        partial_gain_grad = lax.optimization_barrier(jnp.sum(normed_rows_gradient * standardized_rows, axis=0))
        scaled_values = normed_rows_gradient * norm_gain_vector
        final_result = group_cotangent_rows.astype(jnp.float32) + inverse_std * (scaled_values - lax.optimization_barrier(jnp.mean(scaled_values, axis=1, keepdims=True)) - standardized_rows * lax.optimization_barrier(jnp.mean(scaled_values * standardized_rows, axis=1, keepdims=True)))
        return (final_result.astype(jnp.bfloat16), up_part, bias_part, down_part, partial_gain_grad)
    results, up_parts, bias_parts, down_parts, gain_parts = lax.map(group, (packed_in, packed_cot))
    input_grad = results.reshape(TOKENS, D)
    return (input_grad, lax.optimization_barrier(jnp.sum(up_parts, axis=0)), lax.optimization_barrier(jnp.sum(bias_parts, axis=0)), lax.optimization_barrier(jnp.sum(down_parts, axis=0)), lax.optimization_barrier(jnp.sum(gain_parts, axis=0)))
```

```python
import jax
import jax.numpy as jnp
from jax import lax
from jax.sharding import Mesh
from jax.sharding import PartitionSpec as P

DP = ("dp_0", "dp_1")
FSDP = ("fsdp_0", "fsdp_1", "fsdp_2")
ROWS_AXES = ("fsdp_0", "fsdp_1")
DP_FSDP = ("dp_0", "dp_1", "fsdp_0", "fsdp_1", "fsdp_2")


root_two_pi = 0.7978845608
cubic = 0.044715


def side_by_side(arrays, axis, split_dim, concat_dim, along):
    both = jnp.concatenate(arrays, axis=along)
    filled, at, finished = (
        lax.all_to_all(both, axis, split_axis=split_dim, concat_axis=concat_dim, tiled=True),
        0,
        [],
    )
    for a in arrays:
        finished.append(lax.slice_in_dim(filled, at, at + a.shape[along], axis=along))
        at += a.shape[along]
    return tuple(finished)


def gelu_pair(pre):
    inner = root_two_pi * (pre + cubic * pre * pre * pre)
    tangent = jnp.tanh(inner)
    act = 0.5 * pre * (1.0 + tangent)
    slope = 0.5 * (1.0 + tangent) + 0.5 * pre * (1.0 - tangent * tangent) * root_two_pi * (
        1.0 + 3.0 * cubic * pre * pre
    )
    return (act, slope)


def apply_layer_norm(values):
    row_average = jnp.mean(values, axis=1, keepdims=True)
    centered = values - row_average
    variance = jnp.mean(centered * centered, axis=1, keepdims=True)
    inverse_std = 1.0 / jnp.sqrt(variance + 1e-05)
    return (centered * inverse_std, inverse_std)


def shards(tokens, cotangent, routes, norm_gain_vector, up_weight, up_bias, down_weight):
    particle_slot_count = tokens.shape[0]
    dp_size = lax.axis_size(DP)
    capacity = particle_slot_count // dp_size
    up_weight = lax.all_gather(up_weight, "fsdp_2", axis=1, tiled=True)
    down_weight = lax.all_gather(down_weight, "fsdp_2", axis=0, tiled=True)
    up_bias = lax.all_gather(up_bias, "fsdp_2", axis=0, tiled=True)
    target = routes[:, 0]
    matches = (target[:, None] == jnp.arange(dp_size + 1, dtype=jnp.int32)[None, :]).astype(
        jnp.int32
    )
    earlier = jnp.cumsum(matches, axis=0) - matches
    ranked = jnp.sum(earlier * matches, axis=1)
    slot_index = jnp.where(target < dp_size, target * capacity + ranked, -1)
    placing = (
        slot_index[None, :] == jnp.arange(particle_slot_count, dtype=jnp.int32)[:, None]
    ).astype(jnp.bfloat16)
    send_in = jnp.dot(placing, tokens, preferred_element_type=jnp.float32).astype(jnp.bfloat16)
    send_cot = jnp.dot(placing, cotangent, preferred_element_type=jnp.float32).astype(jnp.bfloat16)
    packed_in, packed_cot = side_by_side((send_in, send_cot), DP, 0, 0, 1)
    local_standardized, own_inverse = apply_layer_norm(packed_in.astype(jnp.float32))
    normed_local = (local_standardized * norm_gain_vector).astype(jnp.bfloat16)
    all_cot = lax.all_gather(packed_cot, ROWS_AXES, axis=0, tiled=True)
    gathered_normed_rows = lax.all_gather(normed_local, ROWS_AXES, axis=0, tiled=True)
    pre = jnp.dot(gathered_normed_rows, up_weight, preferred_element_type=jnp.float32) + up_bias
    act_full, slope = gelu_pair(pre)
    act = act_full.astype(jnp.bfloat16)
    act_grad = jnp.einsum("rd,kd->rk", all_cot, down_weight, preferred_element_type=jnp.float32)
    pre_grad = (act_grad * slope).astype(jnp.bfloat16)
    down_part = jnp.einsum("rk,rd->kd", act, all_cot, preferred_element_type=jnp.float32)
    up_part = jnp.einsum(
        "rk,rd->kd", pre_grad, gathered_normed_rows, preferred_element_type=jnp.float32
    )
    bias_part = jnp.sum(pre_grad.astype(jnp.float32), axis=0)
    partial_gain_grad = jnp.sum(up_part * up_weight.T.astype(jnp.float32), axis=0) / norm_gain_vector
    parts = jnp.concatenate([up_part, down_part], axis=1).astype(jnp.bfloat16)
    mine = lax.psum_scatter(parts, "fsdp_2", scatter_dimension=0, tiled=True)
    mine = lax.psum_scatter(mine, DP, scatter_dimension=0, tiled=True)
    whole = lax.all_gather(mine, DP, axis=0, tiled=True).astype(jnp.float32)
    d = up_weight.shape[0]
    up_grad = whole[:, :d].T
    down_grad = whole[:, d:]
    normed_rows_gradient = lax.psum_scatter(
        jnp.einsum("rk,dk->rd", pre_grad, up_weight, preferred_element_type=jnp.float32).astype(
            jnp.bfloat16
        ),
        ROWS_AXES,
        scatter_dimension=0,
        tiled=True,
    ).astype(jnp.float32)
    index = lax.axis_index(FSDP)
    k = bias_part.shape[0] // 2
    wide = jnp.zeros((8, 2 * k), jnp.float32)
    wide = lax.dynamic_update_slice(wide, bias_part[None], (index // 2, 0))
    small = lax.psum(jnp.concatenate([partial_gain_grad, wide.reshape(-1)]), DP_FSDP)
    gain_grad = small[:d]
    bias_grad = lax.dynamic_slice(small[d:], (index * k,), (k,))
    scaled_values = normed_rows_gradient * norm_gain_vector
    final_result = packed_cot.astype(jnp.float32) + own_inverse * (
        scaled_values
        - jnp.mean(scaled_values, axis=1, keepdims=True)
        - local_standardized * jnp.mean(scaled_values * local_standardized, axis=1, keepdims=True)
    )
    return (final_result.astype(jnp.bfloat16), up_grad, bias_grad, down_grad, gain_grad)


def solution(mesh):
    finer = Mesh(
        mesh.devices.reshape(16, 2, 4, 2, 2), ("dp_0", "dp_1", "fsdp_0", "fsdp_1", "fsdp_2")
    )
    return jax.shard_map(
        shards,
        mesh=finer,
        in_specs=(
            P(DP_FSDP, None),
            P(DP_FSDP, None),
            P(DP_FSDP, None),
            P(),
            P(None, FSDP),
            P(FSDP),
            P(FSDP, None),
        ),
        out_specs=(P(DP_FSDP, None), P(None, FSDP), P(FSDP), P(FSDP, None), P()),
        check_vma=False,
    )
```

```python
import jax
import jax.numpy as jnp
from jax import lax
from jax.experimental import pallas as pl
from jax.experimental.pallas import tpu as pltpu
from jax.sharding import Mesh
from jax.sharding import PartitionSpec as P

FSDP = ("fsdp_0", "fsdp_1", "fsdp_2")
DP_FSDP = ("dp_0", "dp_1", "fsdp_0", "fsdp_1", "fsdp_2")
MESH = pl.DeviceIdType.MESH

root_two_pi = 0.7978845608
cubic = 0.044715

NZ, NX = 16, 4
OFFSETS = [0, 1, 15, 2, 14, 3, 13, 4, 12, 5, 11, 6, 10, 7, 9, 8]
CHUNKS = 4
F32, BF16 = jnp.float32, jnp.bfloat16


def gelu_pair(pre):
    inner = root_two_pi * (pre + cubic * pre * pre * pre)
    tangent = jnp.tanh(inner)
    act = 0.5 * pre * (1.0 + tangent)
    slope = 0.5 * (1.0 + tangent) + 0.5 * pre * (1.0 - tangent * tangent) * root_two_pi * (
        1.0 + 3.0 * cubic * pre * pre
    )
    return (act, slope)


def nn(a, b):
    return lax.dot_general(a, b, (((1,), (0,)), ((), ())), preferred_element_type=F32)


def nt(a, b):
    return lax.dot_general(a, b, (((1,), (1,)), ((), ())), preferred_element_type=F32)


def tn(a, b):
    return lax.dot_general(a, b, (((0,), (0,)), ((), ())), preferred_element_type=F32)


def iota(shape, dim):
    return lax.broadcasted_iota(jnp.int32, shape, dim)


def kernel(
    tok, cot, routes, gain, wu_in, bu_in, wd_in,
    dx_out, up_out, down_out, bias_out, gain_out,
    send, land, g, wu, wd, bu, acc, bacc, part, ret, xh, rs, dxs,
    cs, cr, sp, rp, sm, rm, ys, yr, ag,
    small_s, small_r, gs, ar, bs, br, cc_s, cr_r,
    a2a_s, a2a_r, gat_s, gat_r, w_s, w_r, p_s, p_r, cs_s, cs_r,
    rp_s, rp_r, rm_s, rm_r, y_s, y_r, ap_s, ap_r, am_s, am_r,
    sm_s, sm_r, ga_s, ga_r, gb_s, gb_r, gc_s, gc_r,
):
    z, yl = lax.axis_index("dp_0"), lax.axis_index("dp_1")
    x, yh, c = lax.axis_index("fsdp_0"), lax.axis_index("fsdp_1"), lax.axis_index("fsdp_2")
    pending = []

    def zpeer(dz, dy):
        return (lax.rem(z + dz, NZ), (yl + dy) % 2, x, yh, c)

    def xpeer(rx, ry):
        return (z, yl, lax.rem(x + rx, NX), (yh + ry) % 2, c)

    sibling = (z, yl, x, yh, 1 - c)

    def remote(src, dst, ssem, rsem, peer):
        return pltpu.make_async_remote_copy(
            src_ref=src, dst_ref=dst, send_sem=ssem, recv_sem=rsem,
            device_id=peer, device_id_type=MESH,
        )

    def go(copy):
        copy.start()
        pending.append(copy)
        return copy

    barrier = pltpu.get_barrier_semaphore()
    peers = [zpeer(dz, dy) for dz in range(NZ) for dy in range(2) if dz or dy]
    peers += [xpeer(rx, ry) for rx in range(NX) for ry in range(2) if rx or ry]
    peers.append(sibling)
    for peer in peers:
        pl.semaphore_signal(barrier, inc=1, device_id=peer, device_id_type=MESH)

    target = routes[...]
    hot = (iota((40, 128), 0) == target).astype(BF16)
    before = (iota((128, 128), 0) < iota((128, 128), 1)).astype(BF16)
    ranked = jnp.sum(nn(hot, before) * hot.astype(F32), axis=0, keepdims=True).astype(jnp.int32)
    dz = ((target >> 1) - z + NZ) & (NZ - 1)
    pos = jnp.where(dz == 0, 0, jnp.where(dz <= NZ // 2, 2 * dz - 1, 2 * (NZ - dz)))
    dy = ((target & 1) + yl) & 1
    row = jnp.where(target < 2 * NZ, (pos * 2 + dy) * 8 + ranked, -8)
    line = iota((256, 128), 0)
    placed = nn((line == row).astype(BF16), tok[...]) + nn(
        (line == row + 4).astype(BF16), cot[...]
    )
    send[...] = placed.astype(BF16).reshape(32, 8, 1024)
    land[0] = send[0]
    wu[0:256] = wu_in[...]
    wd[0:256] = wd_in[...]
    bu[0] = bu_in[...]

    pl.semaphore_wait(barrier, len(peers))

    a2a = {}
    for t in range(1, 32):
        a2a[t] = go(
            remote(send.at[t], land.at[t], a2a_s.at[t], a2a_r.at[t], zpeer(OFFSETS[t // 2], t % 2))
        )
    weights = [
        go(remote(wu_in, wu.at[256:512], w_s.at[0], w_r.at[0], sibling)),
        go(remote(wd_in, wd.at[256:512], w_s.at[1], w_r.at[1], sibling)),
        go(remote(bu_in, bu.at[1], w_s.at[2], w_r.at[2], sibling)),
    ]

    moves = [
        (0, 1, (0, 1)),
        (0, 6, (1, 0)), (0, 2, (3, 0)),
        (1, 7, (1, 0)), (1, 3, (3, 0)),
        (6, 4, (1, 0)), (3, 5, (3, 0)),
    ]

    def move(k, i):
        src, dst, (rx, ry) = moves[i]
        return remote(
            g.at[k, :, src], g.at[k, :, dst], gat_s.at[k, i], gat_r.at[k, i], xpeer(rx, ry)
        )

    sorter = iota((64, 64), 0)
    column = iota((64, 64), 1)
    wanted = (column // 8) * 4 + (column % 4) + jnp.where(column % 8 >= 4, 32, 0)
    sort = (sorter == wanted).astype(BF16)

    def own(k):
        for t in range(8 * k, 8 * k + 8):
            if t:
                a2a[t].wait_recv()
        rows = nn(sort, land[8 * k : 8 * k + 8].reshape(64, 1024))
        values = rows[0:32]
        centered = values - jnp.mean(values, axis=1, keepdims=True)
        variance = jnp.mean(centered * centered, axis=1, keepdims=True)
        inverse = 1.0 / jnp.sqrt(variance + 1e-05)
        standard = centered * inverse
        xh[k] = standard
        rs[k] = jnp.broadcast_to(inverse, (32, 128))
        g[k, 0, 0] = (standard * gain[...]).astype(BF16)
        g[k, 1, 0] = rows[32:64].astype(BF16)
        for i in range(3):
            go(move(k, i))

    def second(k):
        move(k, 0).wait_recv()
        go(move(k, 3))
        go(move(k, 4))

    def third(k):
        move(k, 1).wait_recv()
        go(move(k, 5))
        move(k, 4).wait_recv()
        go(move(k, 6))

    def compute(k):
        for i in (2, 3, 5, 6):
            move(k, i).wait_recv()
        normed = g[k, 0].reshape(256, 1024)
        outer = g[k, 1].reshape(256, 1024)
        bias = jnp.concatenate([bu[0], bu[1]], axis=1)
        act, slope = gelu_pair(nt(normed, wu[...]) + bias)
        pre_grad = (nt(outer, wd[...]) * slope).astype(BF16)
        act = act.astype(BF16)
        up = tn(pre_grad, normed).reshape(2, 16, 16, 1024)
        down = tn(act, outer).reshape(2, 16, 16, 1024)
        biases = jnp.sum(pre_grad.astype(F32), axis=0, keepdims=True)
        if k == 0:
            acc[:, 0:16] = up
            acc[:, 16:32] = down
            bacc[...] = biases
        else:
            acc[:, 0:16] += up
            acc[:, 16:32] += down
            bacc[...] += biases
        part[k] = nn(pre_grad, wu[...]).astype(BF16).reshape(8, 32, 1024)

    own(0)
    own(1)
    second(0)
    third(0)
    second(1)
    own(2)
    third(1)
    for w in weights:
        w.wait_recv()
    compute(0)
    second(2)
    own(3)
    third(2)
    compute(1)
    second(3)
    third(3)
    compute(2)
    compute(3)

    def across(r, h):
        return remote(cs.at[r, h], cr.at[r, h], cs_s.at[r, h], cs_r.at[r, h], sibling)

    for r in (8, 9, 7, 10, 6, 11, 5, 12, 4, 13, 3, 14, 2, 15, 1, 0):
        o = lax.rem(z + r, NZ)
        for h in range(2):
            cs[r, h] = acc[1, 2 * o + h].astype(BF16)
            go(across(r, h))

    def home(m):
        rx, ry = m // 2, m % 2
        there = ((NX - rx) % NX) * 2 + ry
        return remote(part.at[:, m], ret.at[there], p_s.at[m], p_r.at[there], xpeer(rx, ry))

    for m in (1, 2, 6, 3, 7, 4, 5):
        go(home(m))

    def mine(r, h):
        return acc[0, 2 * lax.rem(z + r, NZ) + h] + cr[r, h].astype(F32)

    def plus(s, h):
        return remote(sp.at[s, h], rp.at[s, h], rp_s.at[s, h], rp_r.at[s, h], zpeer(1, 0))

    def minus(s, h):
        return remote(sm.at[s, h], rm.at[s, h], rm_s.at[s, h], rm_r.at[s, h], zpeer(NZ - 1, 0))

    def ring(s):
        for h in range(2):
            across(8 - s, h).wait_recv()
            value = mine(8 - s, h)
            if s:
                plus(s - 1, h).wait_recv()
                value = value + rp[s - 1, h].astype(F32)
            sp[s, h] = value.astype(BF16)
            go(plus(s, h))
            if s < 7:
                across(9 + s, h).wait_recv()
                value = mine(9 + s, h)
                if s:
                    minus(s - 1, h).wait_recv()
                    value = value + rm[s - 1, h].astype(F32)
                sm[s, h] = value.astype(BF16)
                go(minus(s, h))

    ring(0)
    weighted = jnp.zeros((1, 1024), F32)
    for half in range(2):
        prod = acc[half, 0:16].reshape(256, 1024) * wu[256 * half : 256 * half + 256].astype(F32)
        weighted = weighted + jnp.sum(prod, axis=0, keepdims=True)
    weighted = weighted / gain[...]
    small_s[:, 0:1024] = weighted
    small_s[:, 1024:1280] = bacc[:, 256:512]
    to_sibling = go(remote(small_s, small_r, sm_s.at[0], sm_r.at[0], sibling))
    ring(1)
    to_sibling.wait_recv()
    whole_gain = weighted + small_r[:, 0:1024]
    for j in range(8):
        gs[j] = whole_gain[:, 128 * j : 128 * j + 128]
    bs[:, 128:384] = bacc[:, 0:256] + small_r[:, 1024:1280]
    here = x * 2 + yh

    def there_of(m):
        return lax.rem(x + m // 2, NX) * 2 + (yh + m % 2) % 2

    ar[here] = gs[here]
    for m in range(1, 8):
        go(
            remote(
                gs.at[there_of(m)], ar.at[here], ga_s.at[m], ga_r.at[here], xpeer(m // 2, m % 2)
            )
        )
    ring(2)
    ring(3)
    for m in range(1, 8):
        j = there_of(m)
        remote(gs.at[j], ar.at[j], ga_s.at[m], ga_r.at[j], sibling).wait_recv()
    bs[:, 0:128] = jnp.sum(ar[...], axis=0)
    number = z * 2 + yl
    br[number] = bs[...]
    for t in range(1, 32):
        go(
            remote(
                bs, br.at[number], gb_s.at[t], gb_r.at[number], zpeer(OFFSETS[t // 2], t % 2)
            )
        )
    for s in range(4, 8):
        ring(s)

    def swap(h):
        return remote(ys.at[h], yr.at[h], y_s.at[h], y_r.at[h], zpeer(0, 1))

    for h in range(2):
        across(0, h).wait_recv()
        plus(7, h).wait_recv()
        minus(6, h).wait_recv()
        total = mine(0, h) + rp[7, h].astype(F32) + rm[6, h].astype(F32)
        ys[h] = total.astype(BF16)
        go(swap(h))

    def spread(s, h, sign):
        origin = lax.rem(z + NZ - sign * s, NZ)
        spot = ag.at[2 * origin + h]
        if sign > 0:
            return remote(spot, spot, ap_s.at[s, h], ap_r.at[s, h], zpeer(1, 0))
        return remote(spot, spot, am_s.at[s, h], am_r.at[s, h], zpeer(NZ - 1, 0))

    def arrived(s, h, sign):
        origin = lax.rem(z + NZ - sign * (s + 1), NZ)
        spot = ag.at[2 * origin + h]
        if sign > 0:
            return remote(spot, spot, ap_s.at[s, h], ap_r.at[s, h], zpeer(1, 0))
        return remote(spot, spot, am_s.at[s, h], am_r.at[s, h], zpeer(NZ - 1, 0))

    for h in range(2):
        swap(h).wait_recv()
        ag[2 * z + h] = (ys[h].astype(F32) + yr[h].astype(F32)).astype(BF16)
        go(spread(0, h, 1))
        go(spread(0, h, -1))

    def turn(s):
        for h in range(2):
            for sign in (1, -1):
                if sign > 0 or s < 8:
                    arrived(s - 1, h, sign).wait_recv()
                    if s < (8 if sign > 0 else 7):
                        go(spread(s, h, sign))

    turn(1)
    for t in range(1, 32):
        source = lax.rem(z + OFFSETS[t // 2], NZ) * 2 + (yl + t % 2) % 2
        remote(bs, br.at[source], gb_s.at[t], gb_r.at[source], sibling).wait_recv()
    sums = jnp.sum(br[...], axis=0)
    bias_out[...] = sums[:, 128:384]
    cc_s[...] = sums[:, 0:128]
    cr_r[here] = sums[:, 0:128]
    for m in range(1, 8):
        go(remote(cc_s, cr_r.at[here], gc_s.at[m], gc_r.at[here], xpeer(m // 2, m % 2)))
    for s in range(2, 5):
        turn(s)

    for m in range(1, 8):
        remote(part.at[:, m], ret.at[m], p_s.at[m], p_r.at[m], sibling).wait_recv()
    for k in range(CHUNKS):
        summed = part[k, 0].astype(F32)
        for m in range(1, 8):
            summed = summed + ret[m, k].astype(F32)
        scaled = summed * gain[...]
        standard = xh[k]
        first = jnp.mean(scaled, axis=1, keepdims=True)
        cross = jnp.mean(scaled * standard, axis=1, keepdims=True)
        value = g[k, 1, 0].astype(F32) + rs[k][:, 0:1] * (scaled - first - standard * cross)
        dxs[k] = value.astype(BF16)
        turn(5 + k)

    spot = iota((128, 128), 1)
    tile = spot // 4
    at = tile // 2
    offset = jnp.where(at == 0, 0, jnp.where(at % 2 == 1, (at + 1) // 2, NZ - at // 2))
    source = ((z - offset + NZ) & (NZ - 1)) * 2 + (((tile % 2) + yl) & 1)
    perm = (iota((128, 128), 0) == source * 4 + spot % 4).astype(BF16)
    dx_out[...] = nn(perm, dxs[...].reshape(128, 1024)).astype(BF16)
    up_out[...] = ag[0:16].reshape(256, 1024)
    down_out[...] = ag[16:32].reshape(256, 1024)
    for m in range(1, 8):
        j = there_of(m)
        remote(cc_s, cr_r.at[j], gc_s.at[m], gc_r.at[j], sibling).wait_recv()
    gain_out[...] = cr_r[...].reshape(8, 128)
    for copy in pending:
        copy.wait_send()


def shards(tokens, cotangent, routes, norm_gain_vector, up_weight, up_bias, down_weight):
    vmem, sem = pltpu.VMEM, pltpu.SemaphoreType.DMA
    dx, up, down, bias, gain = pl.pallas_call(
        kernel,
        out_shape=(
            jax.ShapeDtypeStruct((128, 1024), BF16),
            jax.ShapeDtypeStruct((256, 1024), BF16),
            jax.ShapeDtypeStruct((256, 1024), BF16),
            jax.ShapeDtypeStruct((1, 256), F32),
            jax.ShapeDtypeStruct((8, 128), F32),
        ),
        in_specs=[pl.BlockSpec(memory_space=pltpu.VMEM)] * 7,
        out_specs=[pl.BlockSpec(memory_space=pltpu.VMEM)] * 5,
        scratch_shapes=[
            vmem((32, 8, 1024), BF16),
            vmem((32, 8, 1024), BF16),
            vmem((CHUNKS, 2, 8, 32, 1024), BF16),
            vmem((512, 1024), BF16),
            vmem((512, 1024), BF16),
            vmem((2, 1, 256), F32),
            vmem((2, 32, 16, 1024), F32),
            vmem((1, 512), F32),
            vmem((CHUNKS, 8, 32, 1024), BF16),
            vmem((8, CHUNKS, 32, 1024), BF16),
            vmem((CHUNKS, 32, 1024), F32),
            vmem((CHUNKS, 32, 128), F32),
            vmem((CHUNKS, 32, 1024), BF16),
            vmem((16, 2, 16, 1024), BF16),
            vmem((16, 2, 16, 1024), BF16),
            vmem((8, 2, 16, 1024), BF16),
            vmem((8, 2, 16, 1024), BF16),
            vmem((8, 2, 16, 1024), BF16),
            vmem((8, 2, 16, 1024), BF16),
            vmem((2, 16, 1024), BF16),
            vmem((2, 16, 1024), BF16),
            vmem((32, 16, 1024), BF16),
            vmem((1, 1280), F32),
            vmem((1, 1280), F32),
            vmem((8, 1, 128), F32),
            vmem((8, 1, 128), F32),
            vmem((1, 384), F32),
            vmem((32, 1, 384), F32),
            vmem((1, 128), F32),
            vmem((8, 1, 128), F32),
            sem((32,)), sem((32,)),
            sem((CHUNKS, 7)), sem((CHUNKS, 7)),
            sem((3,)), sem((3,)),
            sem((8,)), sem((8,)),
            sem((16, 2)), sem((16, 2)),
            sem((8, 2)), sem((8, 2)), sem((8, 2)), sem((8, 2)),
            sem((2,)), sem((2,)),
            sem((8, 2)), sem((8, 2)), sem((8, 2)), sem((8, 2)),
            sem((1,)), sem((1,)),
            sem((8,)), sem((8,)),
            sem((32,)), sem((32,)),
            sem((8,)), sem((8,)),
        ],
        compiler_params=pltpu.CompilerParams(
            collective_id=0, has_side_effects=True, vmem_limit_bytes=60 * 1024 * 1024
        ),
        name="ffn_backward",
    )(
        tokens,
        cotangent,
        routes.reshape(1, -1),
        norm_gain_vector.reshape(1, -1),
        up_weight.T,
        up_bias.reshape(1, -1),
        down_weight,
    )
    return (
        dx,
        up.T.astype(F32),
        bias.reshape(-1),
        down.astype(F32),
        gain.reshape(-1),
    )


def solution(mesh):
    finer = Mesh(mesh.devices.reshape(NZ, 2, NX, 2, 2), DP_FSDP)
    return jax.shard_map(
        shards,
        mesh=finer,
        in_specs=(
            P(DP_FSDP, None),
            P(DP_FSDP, None),
            P(DP_FSDP, None),
            P(),
            P(None, FSDP),
            P(FSDP),
            P(FSDP, None),
        ),
        out_specs=(P(DP_FSDP, None), P(None, FSDP), P(FSDP), P(FSDP, None), P()),
        check_vma=False,
    )
```

```python
import jax
import jax.numpy as jnp
from jax import lax
from jax.experimental import pallas as pl
from jax.experimental.pallas import tpu as pltpu
from jax.sharding import Mesh
from jax.sharding import PartitionSpec as P

FSDP = ("fsdp_0", "fsdp_1", "fsdp_2")
DP_FSDP = ("dp_0", "dp_1", "fsdp_0", "fsdp_1", "fsdp_2")
MESH = pl.DeviceIdType.MESH

root_two_pi = 0.7978845608
cubic = 0.044715

NZ, NX = 16, 4
OFFSETS = [0, 1, 15, 2, 14, 3, 13, 4, 12, 5, 11, 6, 10, 7, 9, 8]
CHUNKS, SUBS = 8, 4
F32, BF16 = jnp.float32, jnp.bfloat16


def gelu_pair(pre):
    inner = root_two_pi * (pre + cubic * pre * pre * pre)
    tangent = jnp.tanh(inner)
    act = 0.5 * pre * (1.0 + tangent)
    slope = 0.5 * (1.0 + tangent) + 0.5 * pre * (1.0 - tangent * tangent) * root_two_pi * (
        1.0 + 3.0 * cubic * pre * pre
    )
    return (act, slope)


def nn(a, b):
    return lax.dot_general(a, b, (((1,), (0,)), ((), ())), preferred_element_type=F32)


def nt(a, b):
    return lax.dot_general(a, b, (((1,), (1,)), ((), ())), preferred_element_type=F32)


def tn(a, b):
    return lax.dot_general(a, b, (((0,), (0,)), ((), ())), preferred_element_type=F32)


def iota(shape, dim):
    return lax.broadcasted_iota(jnp.int32, shape, dim)


def kernel(
    tok, cot, routes, gain, wu_in, bu_in, wd_in,
    dxs, ag_out, bias_out, gain_out,
    send, land, g, wu, wd, bu, acc, bacc, part, fars, near_s, near_r, ysend, yrecv, xh, rs,
    cs, cr, sp, rp, sm, rm, ys, yr, ag,
    small_s, small_r, gs, ar, bs, br, cc_s, cr_r,
    a2a_s, a2a_r, gat_s, gat_r, w_s, w_r, p_s, p_r, cs_s, cs_r,
    rp_s, rp_r, rm_s, rm_r, y_s, y_r, ap_s, ap_r, am_s, am_r,
    sm_s, sm_r, ga_s, ga_r, gb_s, gb_r, gc_s, gc_r,
):
    z, yl = lax.axis_index("dp_0"), lax.axis_index("dp_1")
    x, yh, c = lax.axis_index("fsdp_0"), lax.axis_index("fsdp_1"), lax.axis_index("fsdp_2")
    pending = []

    def zpeer(dz, dy):
        return (lax.rem(z + dz, NZ), (yl + dy) % 2, x, yh, c)

    def xpeer(rx, ry):
        return (z, yl, lax.rem(x + rx, NX), (yh + ry) % 2, c)

    sibling = (z, yl, x, yh, 1 - c)

    def remote(src, dst, ssem, rsem, peer):
        return pltpu.make_async_remote_copy(
            src_ref=src, dst_ref=dst, send_sem=ssem, recv_sem=rsem,
            device_id=peer, device_id_type=MESH,
        )

    def go(copy):
        copy.start()
        pending.append(copy)
        return copy

    barrier = pltpu.get_barrier_semaphore()
    peers = [zpeer(dz, dy) for dz in range(NZ) for dy in range(2) if dz or dy]
    peers += [xpeer(rx, ry) for rx in range(NX) for ry in range(2) if rx or ry]
    peers.append(sibling)
    for peer in peers:
        pl.semaphore_signal(barrier, inc=1, device_id=peer, device_id_type=MESH)

    target = routes[...]
    hot = (iota((40, 128), 0) == target).astype(BF16)
    before = (iota((128, 128), 0) < iota((128, 128), 1)).astype(BF16)
    ranked = jnp.sum(nn(hot, before) * hot.astype(F32), axis=0, keepdims=True).astype(jnp.int32)
    dz = ((target >> 1) - z + NZ) & (NZ - 1)
    pos = jnp.where(dz == 0, 0, jnp.where(dz <= NZ // 2, 2 * dz - 1, 2 * (NZ - dz)))
    dy = ((target & 1) + yl) & 1
    row = jnp.where(target < 2 * NZ, (pos * 2 + dy) * 8 + ranked, -8)
    line = iota((256, 128), 0)
    placed = nn((line == row).astype(BF16), tok[...]) + nn(
        (line == row + 4).astype(BF16), cot[...]
    )
    send[...] = placed.astype(BF16).reshape(32, 8, 1024)
    land[0] = send[0]
    wd[0:256] = wd_in[...]
    bu[0] = bu_in[...]

    pl.semaphore_wait(barrier, len(peers))

    a2a = {}
    for t in range(1, 32):
        a2a[t] = go(
            remote(send.at[t], land.at[t], a2a_s.at[t], a2a_r.at[t], zpeer(OFFSETS[t // 2], t % 2))
        )
    wu[0:256] = wu_in[...].T
    weights = [
        go(remote(wu.at[0:256], wu.at[256:512], w_s.at[0], w_r.at[0], sibling)),
        go(remote(wd_in, wd.at[256:512], w_s.at[1], w_r.at[1], sibling)),
        go(remote(bu_in, bu.at[1], w_s.at[2], w_r.at[2], sibling)),
    ]

    moves = [
        (0, 1, (0, 1)),
        (0, 6, (1, 0)), (0, 2, (3, 0)),
        (1, 7, (1, 0)), (1, 3, (3, 0)),
        (6, 4, (1, 0)), (3, 5, (3, 0)),
    ]

    def move(k, i):
        src, dst, (rx, ry) = moves[i]
        return remote(
            g.at[k, :, src], g.at[k, :, dst], gat_s.at[k, i], gat_r.at[k, i], xpeer(rx, ry)
        )

    sorter = iota((32, 32), 0)
    column = iota((32, 32), 1)
    wanted = (column // 8) * 4 + (column % 4) + jnp.where(column % 8 >= 4, 16, 0)
    sort = (sorter == wanted).astype(BF16)

    def own(k):
        for t in range(4 * k, 4 * k + 4):
            if t:
                a2a[t].wait_recv()
        rows = nn(sort, land[4 * k : 4 * k + 4].reshape(32, 1024))
        values = rows[0:16]
        centered = values - jnp.mean(values, axis=1, keepdims=True)
        variance = jnp.mean(centered * centered, axis=1, keepdims=True)
        inverse = 1.0 / jnp.sqrt(variance + 1e-05)
        standard = centered * inverse
        xh[k] = standard
        rs[k] = jnp.broadcast_to(inverse, (16, 128))
        g[k, 0, 0] = (standard * gain[...]).astype(BF16)
        g[k, 1, 0] = rows[16:32].astype(BF16)
        for i in range(3):
            go(move(k, i))

    def second(k):
        move(k, 0).wait_recv()
        go(move(k, 3))
        go(move(k, 4))

    def third(k):
        move(k, 1).wait_recv()
        go(move(k, 5))
        move(k, 4).wait_recv()
        go(move(k, 6))

    def compute(j, n):
        for k in range(j, j + n):
            for i in (2, 3, 5, 6):
                move(k, i).wait_recv()
        normed = g[j : j + n, 0].reshape(128 * n, 1024)
        outer = g[j : j + n, 1].reshape(128 * n, 1024)
        bias = jnp.concatenate([bu[0], bu[1]], axis=1)
        act, slope = gelu_pair(nt(normed, wu[...]) + bias)
        pre_grad = (nt(outer, wd[...]) * slope).astype(BF16)
        act = act.astype(BF16)
        up = tn(pre_grad, normed).reshape(2, 32, 8, 1024)
        down = tn(act, outer).reshape(2, 32, 8, 1024)
        biases = jnp.sum(pre_grad.astype(F32), axis=0, keepdims=True)
        if j == 0:
            acc[:, 0:32] = up
            acc[:, 32:64] = down
            bacc[...] = biases
        else:
            acc[:, 0:32] += up
            acc[:, 32:64] += down
            bacc[...] += biases
        part[j : j + n] = nn(pre_grad, wu[...]).astype(BF16).reshape(n, 8, 16, 1024)

    own(0)
    own(1)
    own(2)
    second(0)
    own(3)
    second(1)
    third(0)
    second(2)
    third(1)
    own(4)
    second(3)
    third(2)
    for w in weights:
        w.wait_recv()
    compute(0, 2)
    own(5)
    third(3)
    second(4)
    third(4)
    compute(2, 2)
    own(6)
    second(5)
    third(5)
    second(6)
    own(7)
    compute(4, 2)
    third(6)
    second(7)
    third(7)
    compute(6, 2)

    def across(r):
        return remote(cs.at[r], cr.at[r], cs_s.at[r], cs_r.at[r], sibling)

    for r in (8, 9, 7, 10, 6, 11, 5, 12, 4, 13, 3, 14, 2, 15, 1, 0):
        o = lax.rem(z + r, NZ)
        cs[r] = acc[1, pl.ds(o * SUBS, SUBS)].astype(BF16)
        go(across(r))

    right, left = xpeer(1, 0), xpeer(NX - 1, 0)
    lo, hi = pl.ds(0, 4), pl.ds(4, 4)

    def raw_plus():
        return remote(part.at[hi, 2:4], near_r.at[0, hi], p_s.at[2], p_r.at[2], right)

    def raw_minus():
        return remote(part.at[lo, 6:8], near_r.at[1, lo], p_s.at[3], p_r.at[3], left)

    def far_plus():
        return remote(part.at[lo, 4:6], fars.at[0], p_s.at[0], p_r.at[0], right)

    def far_minus():
        return remote(part.at[hi, 4:6], fars.at[1], p_s.at[1], p_r.at[1], left)

    def sum_plus():
        return remote(near_s.at[0], near_r.at[0, lo], p_s.at[4], p_r.at[4], right)

    def sum_minus():
        return remote(near_s.at[1], near_r.at[1, hi], p_s.at[5], p_r.at[5], left)

    def last_leg():
        return remote(ysend, yrecv, p_s.at[6], p_r.at[6], xpeer(0, 1))

    for copy in (far_plus(), far_minus(), raw_plus(), raw_minus()):
        go(copy)

    def along_plus():
        far_plus().wait_recv()
        near_s[0] = (part[0:4, 2:4].astype(F32) + fars[0].astype(F32)).astype(BF16)
        go(sum_plus())

    def along_minus():
        far_minus().wait_recv()
        near_s[1] = (part[4:8, 6:8].astype(F32) + fars[1].astype(F32)).astype(BF16)
        go(sum_minus())

    def across_y():
        for copy in (raw_plus(), raw_minus(), sum_plus(), sum_minus()):
            copy.wait_recv()
        ysend[...] = (
            part[:, 1].astype(F32) + near_r[0, :, 1].astype(F32) + near_r[1, :, 1].astype(F32)
        ).astype(BF16)
        go(last_leg())

    def mine(r, h):
        return acc[0, SUBS * lax.rem(z + r, NZ) + h] + cr[r, h].astype(F32)

    def plus(s, h):
        return remote(sp.at[s, h], rp.at[s, h], rp_s.at[s, h], rp_r.at[s, h], zpeer(1, 0))

    def minus(s, h):
        return remote(sm.at[s, h], rm.at[s, h], rm_s.at[s, h], rm_r.at[s, h], zpeer(NZ - 1, 0))

    def ring(s):
        across(8 - s).wait_recv()
        if s < 7:
            across(9 + s).wait_recv()
        for h in range(SUBS):
            value = mine(8 - s, h)
            if s:
                plus(s - 1, h).wait_recv()
                value = value + rp[s - 1, h].astype(F32)
            sp[s, h] = value.astype(BF16)
            go(plus(s, h))
            if s < 7:
                value = mine(9 + s, h)
                if s:
                    minus(s - 1, h).wait_recv()
                    value = value + rm[s - 1, h].astype(F32)
                sm[s, h] = value.astype(BF16)
                go(minus(s, h))

    ring(0)
    weighted = jnp.zeros((1, 1024), F32)
    for half in range(2):
        prod = acc[half, 0:32].reshape(256, 1024) * wu[256 * half : 256 * half + 256].astype(F32)
        weighted = weighted + jnp.sum(prod, axis=0, keepdims=True)
    weighted = weighted / gain[...]
    small_s[:, 0:1024] = weighted
    small_s[:, 1024:1280] = bacc[:, 256:512]
    to_sibling = go(remote(small_s, small_r, sm_s.at[0], sm_r.at[0], sibling))
    ring(1)
    to_sibling.wait_recv()
    whole_gain = weighted + small_r[:, 0:1024]
    for j in range(8):
        gs[j] = whole_gain[:, 128 * j : 128 * j + 128]
    bs[:, 128:384] = bacc[:, 0:256] + small_r[:, 1024:1280]
    here = x * 2 + yh

    def there_of(m):
        return lax.rem(x + m // 2, NX) * 2 + (yh + m % 2) % 2

    ar[here] = gs[here]
    for m in range(1, 8):
        go(
            remote(
                gs.at[there_of(m)], ar.at[here], ga_s.at[m], ga_r.at[here], xpeer(m // 2, m % 2)
            )
        )
    ring(2)
    ring(3)
    along_plus()
    ring(4)
    along_minus()
    for m in range(1, 8):
        j = there_of(m)
        remote(gs.at[j], ar.at[j], ga_s.at[m], ga_r.at[j], sibling).wait_recv()
    bs[:, 0:128] = jnp.sum(ar[...], axis=0)
    number = z * 2 + yl
    br[number] = bs[...]
    for t in range(1, 32):
        go(
            remote(
                bs, br.at[number], gb_s.at[t], gb_r.at[number], zpeer(OFFSETS[t // 2], t % 2)
            )
        )
    for s in range(5, 8):
        ring(s)

    def swap(h):
        return remote(ys.at[h], yr.at[h], y_s.at[h], y_r.at[h], zpeer(0, 1))

    across(0).wait_recv()
    for h in range(SUBS):
        plus(7, h).wait_recv()
        minus(6, h).wait_recv()
        total = mine(0, h) + rp[7, h].astype(F32) + rm[6, h].astype(F32)
        ys[h] = total.astype(BF16)
        go(swap(h))
    across_y()

    def spread(s, h, sign):
        origin = lax.rem(z + NZ - sign * s, NZ)
        spot = ag.at[SUBS * origin + h]
        if sign > 0:
            return remote(spot, spot, ap_s.at[s, h], ap_r.at[s, h], zpeer(1, 0))
        return remote(spot, spot, am_s.at[s, h], am_r.at[s, h], zpeer(NZ - 1, 0))

    def arrived(s, h, sign):
        origin = lax.rem(z + NZ - sign * (s + 1), NZ)
        spot = ag.at[SUBS * origin + h]
        if sign > 0:
            return remote(spot, spot, ap_s.at[s, h], ap_r.at[s, h], zpeer(1, 0))
        return remote(spot, spot, am_s.at[s, h], am_r.at[s, h], zpeer(NZ - 1, 0))

    for h in range(SUBS):
        swap(h).wait_recv()
        ag[SUBS * z + h] = (ys[h].astype(F32) + yr[h].astype(F32)).astype(BF16)
        go(spread(0, h, 1))
        go(spread(0, h, -1))

    def turn(s):
        for h in range(SUBS):
            for sign in (1, -1):
                if sign > 0 or s < 8:
                    arrived(s - 1, h, sign).wait_recv()
                    if s < (8 if sign > 0 else 7):
                        go(spread(s, h, sign))

    turn(1)
    for t in range(1, 32):
        source = lax.rem(z + OFFSETS[t // 2], NZ) * 2 + (yl + t % 2) % 2
        remote(bs, br.at[source], gb_s.at[t], gb_r.at[source], sibling).wait_recv()
    sums = jnp.sum(br[...], axis=0)
    bias_out[...] = sums[:, 128:384]
    cc_s[...] = sums[:, 0:128]
    cr_r[here] = sums[:, 0:128]
    for m in range(1, 8):
        go(remote(cc_s, cr_r.at[here], gc_s.at[m], gc_r.at[here], xpeer(m // 2, m % 2)))
    for s in range(2, 5):
        turn(s)

    last_leg().wait_recv()
    for i in range(4):
        k = pl.ds(2 * i, 2)
        summed = (
            part[k, 0].astype(F32)
            + near_r[0, k, 0].astype(F32)
            + near_r[1, k, 0].astype(F32)
            + yrecv[k].astype(F32)
        ).reshape(32, 1024)
        scaled = summed * gain[...]
        standard = xh[k].reshape(32, 1024)
        first = jnp.mean(scaled, axis=1, keepdims=True)
        cross = jnp.mean(scaled * standard, axis=1, keepdims=True)
        inverse = rs[k].reshape(32, 128)[:, 0:1]
        value = g[k, 1, 0].reshape(32, 1024).astype(F32) + inverse * (
            scaled - first - standard * cross
        )
        dxs[k] = value.astype(BF16).reshape(2, 16, 1024)
        turn(5 + i)
    ag_out[...] = ag[...]
    for m in range(1, 8):
        j = there_of(m)
        remote(cc_s, cr_r.at[j], gc_s.at[m], gc_r.at[j], sibling).wait_recv()
    gain_out[...] = cr_r[...].reshape(8, 128)
    for copy in pending:
        copy.wait_send()


def finish(dxs, sums, dx_out, up_out, down_out):
    z, yl = lax.axis_index("dp_0"), lax.axis_index("dp_1")
    spot = iota((128, 128), 1)
    tile = spot // 4
    at = tile // 2
    offset = jnp.where(at == 0, 0, jnp.where(at % 2 == 1, (at + 1) // 2, NZ - at // 2))
    source = ((z - offset + NZ) & (NZ - 1)) * 2 + (((tile % 2) + yl) & 1)
    perm = (iota((128, 128), 0) == source * 4 + spot % 4).astype(BF16)
    dx_out[...] = nn(perm, dxs[...].reshape(128, 1024)).astype(BF16)
    up_out[...] = sums[0:32].reshape(256, 1024).astype(F32).T
    down_out[...] = sums[32:64].reshape(256, 1024).astype(F32)


def shards(tokens, cotangent, routes, norm_gain_vector, up_weight, up_bias, down_weight):
    vmem, sem = pltpu.VMEM, pltpu.SemaphoreType.DMA
    dxs, sums, bias, gain = pl.pallas_call(
        kernel,
        out_shape=(
            jax.ShapeDtypeStruct((CHUNKS, 16, 1024), BF16),
            jax.ShapeDtypeStruct((64, 8, 1024), BF16),
            jax.ShapeDtypeStruct((1, 256), F32),
            jax.ShapeDtypeStruct((8, 128), F32),
        ),
        in_specs=[pl.BlockSpec(memory_space=pltpu.VMEM)] * 7,
        out_specs=[pl.BlockSpec(memory_space=pltpu.VMEM)] * 4,
        scratch_shapes=[
            vmem((32, 8, 1024), BF16),
            vmem((32, 8, 1024), BF16),
            vmem((CHUNKS, 2, 8, 16, 1024), BF16),
            vmem((512, 1024), BF16),
            vmem((512, 1024), BF16),
            vmem((2, 1, 256), F32),
            vmem((2, 64, 8, 1024), F32),
            vmem((1, 512), F32),
            vmem((CHUNKS, 8, 16, 1024), BF16),
            vmem((2, 4, 2, 16, 1024), BF16),
            vmem((2, 4, 2, 16, 1024), BF16),
            vmem((2, CHUNKS, 2, 16, 1024), BF16),
            vmem((CHUNKS, 16, 1024), BF16),
            vmem((CHUNKS, 16, 1024), BF16),
            vmem((CHUNKS, 16, 1024), F32),
            vmem((CHUNKS, 16, 128), F32),
            vmem((16, SUBS, 8, 1024), BF16),
            vmem((16, SUBS, 8, 1024), BF16),
            vmem((8, SUBS, 8, 1024), BF16),
            vmem((8, SUBS, 8, 1024), BF16),
            vmem((8, SUBS, 8, 1024), BF16),
            vmem((8, SUBS, 8, 1024), BF16),
            vmem((SUBS, 8, 1024), BF16),
            vmem((SUBS, 8, 1024), BF16),
            vmem((64, 8, 1024), BF16),
            vmem((1, 1280), F32),
            vmem((1, 1280), F32),
            vmem((8, 1, 128), F32),
            vmem((8, 1, 128), F32),
            vmem((1, 384), F32),
            vmem((32, 1, 384), F32),
            vmem((1, 128), F32),
            vmem((8, 1, 128), F32),
            sem((32,)), sem((32,)),
            sem((CHUNKS, 7)), sem((CHUNKS, 7)),
            sem((3,)), sem((3,)),
            sem((8,)), sem((8,)),
            sem((16,)), sem((16,)),
            sem((8, SUBS)), sem((8, SUBS)), sem((8, SUBS)), sem((8, SUBS)),
            sem((SUBS,)), sem((SUBS,)),
            sem((8, SUBS)), sem((8, SUBS)), sem((8, SUBS)), sem((8, SUBS)),
            sem((1,)), sem((1,)),
            sem((8,)), sem((8,)),
            sem((32,)), sem((32,)),
            sem((8,)), sem((8,)),
        ],
        compiler_params=pltpu.CompilerParams(
            collective_id=0, has_side_effects=True, vmem_limit_bytes=60 * 1024 * 1024
        ),
        name="ffn_backward",
    )(
        tokens,
        cotangent,
        routes.reshape(1, -1),
        norm_gain_vector.reshape(1, -1),
        up_weight,
        up_bias.reshape(1, -1),
        down_weight,
    )
    dx, up, down = pl.pallas_call(
        finish,
        out_shape=(
            jax.ShapeDtypeStruct((128, 1024), BF16),
            jax.ShapeDtypeStruct((1024, 256), F32),
            jax.ShapeDtypeStruct((256, 1024), F32),
        ),
        in_specs=[pl.BlockSpec(memory_space=pltpu.VMEM)] * 2,
        out_specs=[pl.BlockSpec(memory_space=pltpu.VMEM)] * 3,
        name="finish",
    )(dxs, sums)
    return (dx, up, bias.reshape(-1), down, gain.reshape(-1))


def solution(mesh):
    finer = Mesh(mesh.devices.reshape(NZ, 2, NX, 2, 2), DP_FSDP)
    return jax.shard_map(
        shards,
        mesh=finer,
        in_specs=(
            P(DP_FSDP, None),
            P(DP_FSDP, None),
            P(DP_FSDP, None),
            P(),
            P(None, FSDP),
            P(FSDP),
            P(FSDP, None),
        ),
        out_specs=(P(DP_FSDP, None), P(None, FSDP), P(FSDP), P(FSDP, None), P()),
        check_vma=False,
    )
```

```python
import jax
import jax.numpy as jnp
from jax import lax
from jax.experimental import pallas as pl
from jax.experimental.pallas import tpu as pltpu
from jax.sharding import Mesh
from jax.sharding import PartitionSpec as P

FSDP = ("fsdp_0", "fsdp_1", "fsdp_2")
DP_FSDP = ("dp_0", "dp_1", "fsdp_0", "fsdp_1", "fsdp_2")
MESH = pl.DeviceIdType.MESH

root_two_pi = 0.7978845608
cubic = 0.044715

NZ, NX = 16, 4
OFFSETS = [0, 1, 15, 2, 14, 3, 13, 4, 12, 5, 11, 6, 10, 7, 9, 8]
CHUNKS, SUBS = 8, 4
F32, BF16 = jnp.float32, jnp.bfloat16


def gelu_pair(pre):
    inner = root_two_pi * (pre + cubic * pre * pre * pre)
    tangent = jnp.tanh(inner)
    act = 0.5 * pre * (1.0 + tangent)
    slope = 0.5 * (1.0 + tangent) + 0.5 * pre * (1.0 - tangent * tangent) * root_two_pi * (
        1.0 + 3.0 * cubic * pre * pre
    )
    return (act, slope)


def nn(a, b):
    return lax.dot_general(a, b, (((1,), (0,)), ((), ())), preferred_element_type=F32)


def nt(a, b):
    return lax.dot_general(a, b, (((1,), (1,)), ((), ())), preferred_element_type=F32)


def tn(a, b):
    return lax.dot_general(a, b, (((0,), (0,)), ((), ())), preferred_element_type=F32)


def iota(shape, dim):
    return lax.broadcasted_iota(jnp.int32, shape, dim)


def kernel(
    tok, cot, routes, gain, wu_in, bu_in, wd_in,
    dxs, ag_out, bias_out, gain_out,
    send, land, g, wu, wd, bu, acc, bacc, part, fars, near_s, near_r, ysend, yrecv, xh, rs,
    cs, cr, fs, fr, sp, rp, ys, yr, ag,
    small_s, small_r, gs, ar, bs, br, cc_s, cr_r,
    a2a_s, a2a_r, gat_s, gat_r, w_s, w_r, p_s, p_r, cs_s, cs_r,
    fd_s, fd_r, rp_s, rp_r, y_s, y_r, ap_s, ap_r, am_s, am_r,
    sm_s, sm_r, ga_s, ga_r, gb_s, gb_r, gc_s, gc_r,
):
    z, yl = lax.axis_index("dp_0"), lax.axis_index("dp_1")
    x, yh, c = lax.axis_index("fsdp_0"), lax.axis_index("fsdp_1"), lax.axis_index("fsdp_2")
    pending = []

    def zpeer(dz, dy):
        return (lax.rem(z + dz, NZ), (yl + dy) % 2, x, yh, c)

    def xpeer(rx, ry):
        return (z, yl, lax.rem(x + rx, NX), (yh + ry) % 2, c)

    sibling = (z, yl, x, yh, 1 - c)

    def remote(src, dst, ssem, rsem, peer):
        return pltpu.make_async_remote_copy(
            src_ref=src, dst_ref=dst, send_sem=ssem, recv_sem=rsem,
            device_id=peer, device_id_type=MESH,
        )

    def go(copy):
        copy.start()
        pending.append(copy)
        return copy

    barrier = pltpu.get_barrier_semaphore()
    peers = [zpeer(dz, dy) for dz in range(NZ) for dy in range(2) if dz or dy]
    peers += [xpeer(rx, ry) for rx in range(NX) for ry in range(2) if rx or ry]
    peers.append(sibling)
    for peer in peers:
        pl.semaphore_signal(barrier, inc=1, device_id=peer, device_id_type=MESH)

    target = routes[...]
    hot = (iota((40, 128), 0) == target).astype(BF16)
    before = (iota((128, 128), 0) < iota((128, 128), 1)).astype(BF16)
    ranked = jnp.sum(nn(hot, before) * hot.astype(F32), axis=0, keepdims=True).astype(jnp.int32)
    dz = ((target >> 1) - z + NZ) & (NZ - 1)
    pos = jnp.where(dz == 0, 0, jnp.where(dz <= NZ // 2, 2 * dz - 1, 2 * (NZ - dz)))
    dy = ((target & 1) + yl) & 1
    row = jnp.where(target < 2 * NZ, (pos * 2 + dy) * 8 + ranked, -8)
    line = iota((256, 128), 0)
    placed = nn((line == row).astype(BF16), tok[...]) + nn(
        (line == row + 4).astype(BF16), cot[...]
    )
    send[...] = placed.astype(BF16).reshape(32, 8, 1024)
    land[0] = send[0]
    wd[0:256] = wd_in[...]
    bu[0] = bu_in[...]

    pl.semaphore_wait(barrier, len(peers))

    a2a = {}
    for t in range(1, 32):
        a2a[t] = go(
            remote(send.at[t], land.at[t], a2a_s.at[t], a2a_r.at[t], zpeer(OFFSETS[t // 2], t % 2))
        )
    weights = [
        (remote(wu.at[0:256], wu.at[256:512], w_s.at[0], w_r.at[0], sibling)),
        (remote(wd_in, wd.at[256:512], w_s.at[1], w_r.at[1], sibling)),
        (remote(bu_in, bu.at[1], w_s.at[2], w_r.at[2], sibling)),
    ]

    STAGED_Y, STAGED_X, DIRECT = 0, 1, 2
    plan = [STAGED_Y, STAGED_X, STAGED_Y, STAGED_X, STAGED_Y, STAGED_X, STAGED_X, DIRECT]
    here_now = set()

    def push(k, src, dst, rx, ry):
        go(
            remote(
                g.at[k, :, src], g.at[k, :, dst], gat_s.at[k, dst], gat_r.at[k, dst], xpeer(rx, ry)
            )
        )

    def need(k, slot):
        if (k, slot) not in here_now:
            here_now.add((k, slot))
            spot = g.at[k, :, slot]
            remote(spot, spot, gat_s.at[k, slot], gat_r.at[k, slot], sibling).wait_recv()

    sorter = iota((32, 32), 0)
    column = iota((32, 32), 1)
    wanted = (column // 8) * 4 + (column % 4) + jnp.where(column % 8 >= 4, 16, 0)
    sort = (sorter == wanted).astype(BF16)

    def own(k):
        for t in range(4 * k, 4 * k + 4):
            if t:
                a2a[t].wait_recv()
        rows = nn(sort, land[4 * k : 4 * k + 4].reshape(32, 1024))
        values = rows[0:16]
        centered = values - jnp.mean(values, axis=1, keepdims=True)
        variance = jnp.mean(centered * centered, axis=1, keepdims=True)
        inverse = 1.0 / jnp.sqrt(variance + 1e-05)
        standard = centered * inverse
        xh[k] = standard
        rs[k] = jnp.broadcast_to(inverse, (16, 128))
        g[k, 0, 0] = (standard * gain[...]).astype(BF16)
        g[k, 1, 0] = rows[16:32].astype(BF16)
        if plan[k] == STAGED_Y:
            push(k, 0, 1, 0, 1)
            push(k, 0, 6, 1, 0)
            push(k, 0, 2, 3, 0)
        elif plan[k] == STAGED_X:
            push(k, 0, 4, 2, 0)
            push(k, 0, 6, 1, 0)
            push(k, 0, 2, 3, 0)
            push(k, 0, 1, 0, 1)
        else:
            for rx, ry in ((2, 1), (1, 1), (3, 1), (0, 1), (2, 0), (1, 0), (3, 0)):
                push(k, 0, ((NX - rx) % NX) * 2 + ry, rx, ry)

    def second(k):
        if plan[k] == STAGED_Y:
            need(k, 1)
            push(k, 1, 7, 1, 0)
            push(k, 1, 3, 3, 0)
        else:
            for slot in (6, 2, 4):
                need(k, slot)
                push(k, slot, slot + 1, 0, 1)

    def third(k):
        need(k, 6)
        push(k, 6, 4, 1, 0)
        need(k, 3)
        push(k, 3, 5, 3, 0)

    def compute(j, n):
        for k in range(j, j + n):
            for slot in range(1, 8):
                need(k, slot)
        normed = g[j : j + n, 0].reshape(128 * n, 1024)
        outer = g[j : j + n, 1].reshape(128 * n, 1024)
        bias = jnp.concatenate([bu[0], bu[1]], axis=1)
        act, slope = gelu_pair(nt(normed, wu[...]) + bias)
        pre_grad = (nt(outer, wd[...]) * slope).astype(BF16)
        act = act.astype(BF16)
        up = tn(pre_grad, normed).reshape(2, 32, 8, 1024)
        down = tn(act, outer).reshape(2, 32, 8, 1024)
        biases = jnp.sum(pre_grad.astype(F32), axis=0, keepdims=True)
        if j == 0:
            acc[:, 0:32] = up
            acc[:, 32:64] = down
            bacc[...] = biases
        else:
            acc[:, 0:32] += up
            acc[:, 32:64] += down
            bacc[...] += biases
        part[j : j + n] = nn(pre_grad, wu[...]).astype(BF16).reshape(n, 8, 16, 1024)

    own(0)
    own(1)
    own(2)
    second(0)
    own(3)
    wu[0:256] = wu_in[...].T
    for w in weights:
        go(w)
    second(1)
    second(2)
    third(0)
    own(4)
    second(3)
    third(2)
    for w in weights:
        w.wait_recv()
    compute(0, 2)
    own(5)
    second(4)
    compute(2, 2)
    third(4)
    own(6)
    second(5)
    own(7)
    second(6)
    compute(4, 2)
    compute(6, 1)
    compute(7, 1)

    def across(r):
        return remote(cs.at[r], cr.at[r], cs_s.at[r], cs_r.at[r], sibling)

    for r in (8, 7, 9, 5, 11, 6, 10, 3, 13, 4, 12, 1, 15, 2, 14, 0):
        o = lax.rem(z + r, NZ)
        cs[r] = acc[1, pl.ds(o * SUBS, SUBS)].astype(BF16)
        go(across(r))

    right, left = xpeer(1, 0), xpeer(NX - 1, 0)
    lo, hi = pl.ds(0, 4), pl.ds(4, 4)

    def raw_plus():
        return remote(part.at[hi, 2:4], near_r.at[0, hi], p_s.at[2], p_r.at[2], right)

    def raw_minus():
        return remote(part.at[lo, 6:8], near_r.at[1, lo], p_s.at[3], p_r.at[3], left)

    def far_plus():
        return remote(part.at[lo, 4:6], fars.at[0], p_s.at[0], p_r.at[0], right)

    def far_minus():
        return remote(part.at[hi, 4:6], fars.at[1], p_s.at[1], p_r.at[1], left)

    def sum_plus():
        return remote(near_s.at[0], near_r.at[0, lo], p_s.at[4], p_r.at[4], right)

    def sum_minus():
        return remote(near_s.at[1], near_r.at[1, hi], p_s.at[5], p_r.at[5], left)

    def last_leg():
        return remote(ysend, yrecv, p_s.at[6], p_r.at[6], xpeer(0, 1))

    for copy in (far_plus(), far_minus(), raw_plus(), raw_minus()):
        go(copy)

    def along_plus():
        far_plus().wait_recv()
        near_s[0] = (part[0:4, 2:4].astype(F32) + fars[0].astype(F32)).astype(BF16)
        go(sum_plus())

    def along_minus():
        far_minus().wait_recv()
        near_s[1] = (part[4:8, 6:8].astype(F32) + fars[1].astype(F32)).astype(BF16)
        go(sum_minus())

    def across_y():
        for copy in (raw_plus(), raw_minus(), sum_plus(), sum_minus()):
            copy.wait_recv()
        ysend[...] = (
            part[:, 1].astype(F32) + near_r[0, :, 1].astype(F32) + near_r[1, :, 1].astype(F32)
        ).astype(BF16)
        go(last_leg())

    def mine(r, h):
        return acc[0, SUBS * lax.rem(z + r, NZ) + h] + cr[r, h].astype(F32)

    ways = (0, 1)

    def toward(way, d):
        return d if way == 0 else NZ - d

    def feed(way, d):
        return remote(
            fs.at[way, d // 2], fr.at[way, d // 2], fd_s.at[way, d // 2], fd_r.at[way, d // 2],
            zpeer(toward(way, 1), 0),
        )

    def chain(way, d, h):
        i = d // 2 - 1
        return remote(
            sp.at[way, i, h], rp.at[way, i, h], rp_s.at[way, i, h], rp_r.at[way, i, h],
            zpeer(toward(way, 2), 0),
        )

    def feeders(d):
        for way in ways:
            r = toward(way, d)
            across(r).wait_recv()
            for h in range(SUBS):
                fs[way, d // 2, h] = mine(r, h).astype(BF16)
            go(feed(way, d))

    def links(d):
        for way in ways:
            if d == 8 and way:
                continue
            across(toward(way, d)).wait_recv()
            if d < 8:
                feed(way, d + 1).wait_recv()
        for h in range(SUBS):
            for way in ways:
                if d == 8 and way:
                    continue
                value = mine(toward(way, d), h)
                if d < 8:
                    value = value + fr[way, d // 2, h].astype(F32)
                if d < (8 if way == 0 else 6):
                    chain(way, d + 2, h).wait_recv()
                    value = value + rp[way, d // 2, h].astype(F32)
                sp[way, d // 2 - 1, h] = value.astype(BF16)
                go(chain(way, d, h))

    links(8)
    feeders(7)
    feeders(5)
    weighted = jnp.zeros((1, 1024), F32)
    for half in range(2):
        prod = acc[half, 0:32].reshape(256, 1024) * wu[256 * half : 256 * half + 256].astype(F32)
        weighted = weighted + jnp.sum(prod, axis=0, keepdims=True)
    weighted = weighted / gain[...]
    small_s[:, 0:1024] = weighted
    small_s[:, 1024:1280] = bacc[:, 256:512]
    to_sibling = go(remote(small_s, small_r, sm_s.at[0], sm_r.at[0], sibling))
    links(6)
    feeders(3)
    to_sibling.wait_recv()
    whole_gain = weighted + small_r[:, 0:1024]
    for j in range(8):
        gs[j] = whole_gain[:, 128 * j : 128 * j + 128]
    bs[:, 128:384] = bacc[:, 0:256] + small_r[:, 1024:1280]
    here = x * 2 + yh

    def there_of(m):
        return lax.rem(x + m // 2, NX) * 2 + (yh + m % 2) % 2

    ar[here] = gs[here]
    for m in range(1, 8):
        go(
            remote(
                gs.at[there_of(m)], ar.at[here], ga_s.at[m], ga_r.at[here], xpeer(m // 2, m % 2)
            )
        )
    links(4)
    feeders(1)
    along_plus()
    along_minus()
    for m in range(1, 8):
        j = there_of(m)
        remote(gs.at[j], ar.at[j], ga_s.at[m], ga_r.at[j], sibling).wait_recv()
    bs[:, 0:128] = jnp.sum(ar[...], axis=0)
    number = z * 2 + yl
    br[number] = bs[...]
    for t in range(1, 32):
        go(
            remote(
                bs, br.at[number], gb_s.at[t], gb_r.at[number], zpeer(OFFSETS[t // 2], t % 2)
            )
        )
    links(2)

    def swap(h):
        return remote(ys.at[h], yr.at[h], y_s.at[h], y_r.at[h], zpeer(0, 1))

    across(0).wait_recv()
    for way in ways:
        feed(way, 1).wait_recv()
    for h in range(SUBS):
        total = mine(0, h)
        for way in ways:
            chain(way, 2, h).wait_recv()
            total = total + rp[way, 0, h].astype(F32) + fr[way, 0, h].astype(F32)
        ys[h] = total.astype(BF16)
        go(swap(h))

    def spots(way, d, h, n):
        origin = lax.rem(z + toward(1 - way, d), NZ)
        return ag.at[pl.ds(SUBS * origin + h, n)]

    def stride(way, d, h, at):
        spot = spots(way, at, h, 1)
        i = d // 2 - 1
        return remote(
            spot, spot, ap_s.at[way, i, h], ap_r.at[way, i, h], zpeer(toward(way, 2), 0)
        )

    def single(way, d, at):
        spot = spots(way, at, 0, SUBS)
        i = d // 2
        return remote(spot, spot, am_s.at[way, i], am_r.at[way, i], zpeer(toward(way, 1), 0))

    for h in range(SUBS):
        swap(h).wait_recv()
        ag[SUBS * z + h] = (ys[h].astype(F32) + yr[h].astype(F32)).astype(BF16)
        for way in ways:
            go(stride(way, 2, h, 0))
    for way in ways:
        go(single(way, 1, 0))
    across_y()

    def turn(d):
        for h in range(SUBS):
            for way in ways:
                stride(way, d, h, d).wait_recv()
                if d < (8 if way == 0 else 6):
                    go(stride(way, d + 2, h, d))
        for way in ways:
            go(single(way, d + 1, d))

    for t in range(1, 32):
        source = lax.rem(z + OFFSETS[t // 2], NZ) * 2 + (yl + t % 2) % 2
        remote(bs, br.at[source], gb_s.at[t], gb_r.at[source], sibling).wait_recv()
    sums = jnp.sum(br[...], axis=0)
    bias_out[...] = sums[:, 128:384]
    cc_s[...] = sums[:, 0:128]
    cr_r[here] = sums[:, 0:128]
    for m in range(1, 8):
        go(remote(cc_s, cr_r.at[here], gc_s.at[m], gc_r.at[here], xpeer(m // 2, m % 2)))
    turn(2)
    turn(4)
    turn(6)

    last_leg().wait_recv()
    for i in range(4):
        k = pl.ds(2 * i, 2)
        summed = (
            part[k, 0].astype(F32)
            + near_r[0, k, 0].astype(F32)
            + near_r[1, k, 0].astype(F32)
            + yrecv[k].astype(F32)
        ).reshape(32, 1024)
        scaled = summed * gain[...]
        standard = xh[k].reshape(32, 1024)
        first = jnp.mean(scaled, axis=1, keepdims=True)
        cross = jnp.mean(scaled * standard, axis=1, keepdims=True)
        inverse = rs[k].reshape(32, 128)[:, 0:1]
        value = g[k, 1, 0].reshape(32, 1024).astype(F32) + inverse * (
            scaled - first - standard * cross
        )
        dxs[k] = value.astype(BF16).reshape(2, 16, 1024)
    for way in ways:
        for d in (1, 3, 5, 7):
            single(way, d, d).wait_recv()
    for h in range(SUBS):
        stride(0, 8, h, 8).wait_recv()
    ag_out[...] = ag[...]
    for m in range(1, 8):
        j = there_of(m)
        remote(cc_s, cr_r.at[j], gc_s.at[m], gc_r.at[j], sibling).wait_recv()
    gain_out[...] = cr_r[...].reshape(8, 128)
    for copy in pending:
        copy.wait_send()


def finish(dxs, sums, dx_out, up_out, down_out):
    z, yl = lax.axis_index("dp_0"), lax.axis_index("dp_1")
    spot = iota((128, 128), 1)
    tile = spot // 4
    at = tile // 2
    offset = jnp.where(at == 0, 0, jnp.where(at % 2 == 1, (at + 1) // 2, NZ - at // 2))
    source = ((z - offset + NZ) & (NZ - 1)) * 2 + (((tile % 2) + yl) & 1)
    perm = (iota((128, 128), 0) == source * 4 + spot % 4).astype(BF16)
    dx_out[...] = nn(perm, dxs[...].reshape(128, 1024)).astype(BF16)
    up_out[...] = sums[0:32].reshape(256, 1024).astype(F32).T
    down_out[...] = sums[32:64].reshape(256, 1024).astype(F32)


def shards(tokens, cotangent, routes, norm_gain_vector, up_weight, up_bias, down_weight):
    vmem, sem = pltpu.VMEM, pltpu.SemaphoreType.DMA
    dxs, sums, bias, gain = pl.pallas_call(
        kernel,
        out_shape=(
            jax.ShapeDtypeStruct((CHUNKS, 16, 1024), BF16),
            jax.ShapeDtypeStruct((64, 8, 1024), BF16),
            jax.ShapeDtypeStruct((1, 256), F32),
            jax.ShapeDtypeStruct((8, 128), F32),
        ),
        in_specs=[pl.BlockSpec(memory_space=pltpu.VMEM)] * 7,
        out_specs=[pl.BlockSpec(memory_space=pltpu.VMEM)] * 4,
        scratch_shapes=[
            vmem((32, 8, 1024), BF16),
            vmem((32, 8, 1024), BF16),
            vmem((CHUNKS, 2, 8, 16, 1024), BF16),
            vmem((512, 1024), BF16),
            vmem((512, 1024), BF16),
            vmem((2, 1, 256), F32),
            vmem((2, 64, 8, 1024), F32),
            vmem((1, 512), F32),
            vmem((CHUNKS, 8, 16, 1024), BF16),
            vmem((2, 4, 2, 16, 1024), BF16),
            vmem((2, 4, 2, 16, 1024), BF16),
            vmem((2, CHUNKS, 2, 16, 1024), BF16),
            vmem((CHUNKS, 16, 1024), BF16),
            vmem((CHUNKS, 16, 1024), BF16),
            vmem((CHUNKS, 16, 1024), F32),
            vmem((CHUNKS, 16, 128), F32),
            vmem((16, SUBS, 8, 1024), BF16),
            vmem((16, SUBS, 8, 1024), BF16),
            vmem((2, 4, SUBS, 8, 1024), BF16),
            vmem((2, 4, SUBS, 8, 1024), BF16),
            vmem((2, 4, SUBS, 8, 1024), BF16),
            vmem((2, 4, SUBS, 8, 1024), BF16),
            vmem((SUBS, 8, 1024), BF16),
            vmem((SUBS, 8, 1024), BF16),
            vmem((64, 8, 1024), BF16),
            vmem((1, 1280), F32),
            vmem((1, 1280), F32),
            vmem((8, 1, 128), F32),
            vmem((8, 1, 128), F32),
            vmem((1, 384), F32),
            vmem((32, 1, 384), F32),
            vmem((1, 128), F32),
            vmem((8, 1, 128), F32),
            sem((32,)), sem((32,)),
            sem((CHUNKS, 8)), sem((CHUNKS, 8)),
            sem((3,)), sem((3,)),
            sem((8,)), sem((8,)),
            sem((16,)), sem((16,)),
            sem((2, 4)), sem((2, 4)),
            sem((2, 4, SUBS)), sem((2, 4, SUBS)),
            sem((SUBS,)), sem((SUBS,)),
            sem((2, 4, SUBS)), sem((2, 4, SUBS)),
            sem((2, 4)), sem((2, 4)),
            sem((1,)), sem((1,)),
            sem((8,)), sem((8,)),
            sem((32,)), sem((32,)),
            sem((8,)), sem((8,)),
        ],
        compiler_params=pltpu.CompilerParams(
            collective_id=0, has_side_effects=True, vmem_limit_bytes=60 * 1024 * 1024
        ),
        name="ffn_backward",
    )(
        tokens,
        cotangent,
        routes.reshape(1, -1),
        norm_gain_vector.reshape(1, -1),
        up_weight,
        up_bias.reshape(1, -1),
        down_weight,
    )
    dx, up, down = pl.pallas_call(
        finish,
        out_shape=(
            jax.ShapeDtypeStruct((128, 1024), BF16),
            jax.ShapeDtypeStruct((1024, 256), F32),
            jax.ShapeDtypeStruct((256, 1024), F32),
        ),
        in_specs=[pl.BlockSpec(memory_space=pltpu.VMEM)] * 2,
        out_specs=[pl.BlockSpec(memory_space=pltpu.VMEM)] * 3,
        name="finish",
    )(dxs, sums)
    return (dx, up, bias.reshape(-1), down, gain.reshape(-1))


def solution(mesh):
    finer = Mesh(mesh.devices.reshape(NZ, 2, NX, 2, 2), DP_FSDP)
    return jax.shard_map(
        shards,
        mesh=finer,
        in_specs=(
            P(DP_FSDP, None),
            P(DP_FSDP, None),
            P(DP_FSDP, None),
            P(),
            P(None, FSDP),
            P(FSDP),
            P(FSDP, None),
        ),
        out_specs=(P(DP_FSDP, None), P(None, FSDP), P(FSDP), P(FSDP, None), P()),
        check_vma=False,
    )
```

```python
import jax
import jax.numpy as jnp
from jax import lax
from jax.experimental import pallas as pl
from jax.experimental.pallas import tpu as pltpu
from jax.sharding import Mesh
from jax.sharding import PartitionSpec as P

FSDP = ("fsdp_0", "fsdp_1", "fsdp_2")
DP_FSDP = ("dp_0", "dp_1", "fsdp_0", "fsdp_1", "fsdp_2")
MESH = pl.DeviceIdType.MESH

root_two_pi = 0.7978845608
cubic = 0.044715

NZ, NX = 16, 4
OFFSETS = [0, 1, 15, 2, 14, 3, 13, 4, 12, 5, 11, 6, 10, 7, 9, 8]
CHUNKS, SUBS = 8, 4
F32, BF16 = jnp.float32, jnp.bfloat16


def gelu_pair(pre):
    inner = root_two_pi * (pre + cubic * pre * pre * pre)
    tangent = jnp.tanh(inner)
    act = 0.5 * pre * (1.0 + tangent)
    slope = 0.5 * (1.0 + tangent) + 0.5 * pre * (1.0 - tangent * tangent) * root_two_pi * (
        1.0 + 3.0 * cubic * pre * pre
    )
    return (act, slope)


def nn(a, b):
    return lax.dot_general(a, b, (((1,), (0,)), ((), ())), preferred_element_type=F32)


def nt(a, b):
    return lax.dot_general(a, b, (((1,), (1,)), ((), ())), preferred_element_type=F32)


def tn(a, b):
    return lax.dot_general(a, b, (((0,), (0,)), ((), ())), preferred_element_type=F32)


def iota(shape, dim):
    return lax.broadcasted_iota(jnp.int32, shape, dim)


def kernel(
    tok, cot, routes, gain, wu_in, bu_in, wd_in,
    dxs, ag_out, bias_out, gain_out,
    send, land, g, wu, wd, bu, acc, bacc, part, fars, near_s, near_r, ysend, yrecv, xh, rs,
    cs, cr, fs, fr, sp, rp, ys, yr, ag,
    small_s, small_r, gs, ar, bs, br, cc_s, cr_r,
    a2a_s, a2a_r, gat_s, gat_r, w_s, w_r, p_s, p_r, cs_s, cs_r,
    fd_s, fd_r, rp_s, rp_r, y_s, y_r, ap_s, ap_r, am_s, am_r,
    sm_s, sm_r, ga_s, ga_r, gb_s, gb_r, gc_s, gc_r,
):
    z, yl = lax.axis_index("dp_0"), lax.axis_index("dp_1")
    x, yh, c = lax.axis_index("fsdp_0"), lax.axis_index("fsdp_1"), lax.axis_index("fsdp_2")
    pending = []

    def zpeer(dz, dy):
        return (lax.rem(z + dz, NZ), (yl + dy) % 2, x, yh, c)

    def xpeer(rx, ry):
        return (z, yl, lax.rem(x + rx, NX), (yh + ry) % 2, c)

    sibling = (z, yl, x, yh, 1 - c)

    def remote(src, dst, ssem, rsem, peer):
        return pltpu.make_async_remote_copy(
            src_ref=src, dst_ref=dst, send_sem=ssem, recv_sem=rsem,
            device_id=peer, device_id_type=MESH,
        )

    def go(copy):
        copy.start()
        pending.append(copy)
        return copy

    barrier = pltpu.get_barrier_semaphore()
    peers = [zpeer(dz, dy) for dz in range(NZ) for dy in range(2) if dz or dy]
    peers += [xpeer(rx, ry) for rx in range(NX) for ry in range(2) if rx or ry]
    peers.append(sibling)
    for peer in peers:
        pl.semaphore_signal(barrier, inc=1, device_id=peer, device_id_type=MESH)

    target = routes[...]
    hot = (iota((40, 128), 0) == target).astype(BF16)
    before = (iota((128, 128), 0) < iota((128, 128), 1)).astype(BF16)
    ranked = jnp.sum(nn(hot, before) * hot.astype(F32), axis=0, keepdims=True).astype(jnp.int32)
    dz = ((target >> 1) - z + NZ) & (NZ - 1)
    pos = jnp.where(dz == 0, 0, jnp.where(dz <= NZ // 2, 2 * dz - 1, 2 * (NZ - dz)))
    dy = ((target & 1) + yl) & 1
    row = jnp.where(target < 2 * NZ, (pos * 2 + dy) * 8 + ranked, -8)
    line = iota((256, 128), 0)
    placed = nn((line == row).astype(BF16), tok[...]) + nn(
        (line == row + 4).astype(BF16), cot[...]
    )
    send[...] = placed.astype(BF16).reshape(32, 8, 1024)
    land[0] = send[0]
    wd[0:256] = wd_in[...]
    bu[0] = bu_in[...]

    pl.semaphore_wait(barrier, len(peers))

    a2a = {}
    for t in range(1, 32):
        a2a[t] = go(
            remote(send.at[t], land.at[t], a2a_s.at[t], a2a_r.at[t], zpeer(OFFSETS[t // 2], t % 2))
        )
    weights = [
        (remote(wu.at[0:256], wu.at[256:512], w_s.at[0], w_r.at[0], sibling)),
        (remote(wd_in, wd.at[256:512], w_s.at[1], w_r.at[1], sibling)),
        (remote(bu_in, bu.at[1], w_s.at[2], w_r.at[2], sibling)),
    ]

    STAGED_Y, STAGED_X, DIRECT = 0, 1, 2
    plan = [STAGED_Y, STAGED_X, STAGED_Y, STAGED_Y, STAGED_X, STAGED_Y, STAGED_Y, DIRECT]
    here_now = set()

    def push(k, src, dst, rx, ry):
        go(
            remote(
                g.at[k, :, src], g.at[k, :, dst], gat_s.at[k, dst], gat_r.at[k, dst], xpeer(rx, ry)
            )
        )

    def need(k, slot):
        if (k, slot) not in here_now:
            here_now.add((k, slot))
            spot = g.at[k, :, slot]
            remote(spot, spot, gat_s.at[k, slot], gat_r.at[k, slot], sibling).wait_recv()

    sorter = iota((32, 32), 0)
    column = iota((32, 32), 1)
    wanted = (column // 8) * 4 + (column % 4) + jnp.where(column % 8 >= 4, 16, 0)
    sort = (sorter == wanted).astype(BF16)

    def own(k):
        for t in range(4 * k, 4 * k + 4):
            if t:
                a2a[t].wait_recv()
        rows = nn(sort, land[4 * k : 4 * k + 4].reshape(32, 1024))
        values = rows[0:16]
        centered = values - jnp.mean(values, axis=1, keepdims=True)
        variance = jnp.mean(centered * centered, axis=1, keepdims=True)
        inverse = 1.0 / jnp.sqrt(variance + 1e-05)
        standard = centered * inverse
        xh[k] = standard
        rs[k] = jnp.broadcast_to(inverse, (16, 128))
        g[k, 0, 0] = (standard * gain[...]).astype(BF16)
        g[k, 1, 0] = rows[16:32].astype(BF16)
        if plan[k] == STAGED_Y:
            push(k, 0, 1, 0, 1)
            push(k, 0, 6, 1, 0)
            push(k, 0, 2, 3, 0)
        elif plan[k] == STAGED_X:
            push(k, 0, 4, 2, 0)
            push(k, 0, 6, 1, 0)
            push(k, 0, 2, 3, 0)
            push(k, 0, 1, 0, 1)
        else:
            for rx, ry in ((2, 1), (1, 1), (3, 1), (0, 1), (2, 0), (1, 0), (3, 0)):
                push(k, 0, ((NX - rx) % NX) * 2 + ry, rx, ry)

    def second(k):
        if plan[k] == STAGED_Y:
            need(k, 1)
            push(k, 1, 7, 1, 0)
            push(k, 1, 3, 3, 0)
        else:
            for slot in (6, 2, 4):
                need(k, slot)
                push(k, slot, slot + 1, 0, 1)

    def third(k):
        need(k, 6)
        push(k, 6, 4, 1, 0)
        need(k, 3)
        push(k, 3, 5, 3, 0)

    def compute(j, n):
        for k in range(j, j + n):
            for slot in range(1, 8):
                need(k, slot)
        normed = g[j : j + n, 0].reshape(128 * n, 1024)
        outer = g[j : j + n, 1].reshape(128 * n, 1024)
        bias = jnp.concatenate([bu[0], bu[1]], axis=1)
        act, slope = gelu_pair(nt(normed, wu[...]) + bias)
        pre_grad = (nt(outer, wd[...]) * slope).astype(BF16)
        act = act.astype(BF16)
        up = tn(pre_grad, normed).reshape(2, 32, 8, 1024)
        down = tn(act, outer).reshape(2, 32, 8, 1024)
        biases = jnp.sum(pre_grad.astype(F32), axis=0, keepdims=True)
        if j == 0:
            acc[:, 0:32] = up
            acc[:, 32:64] = down
            bacc[...] = biases
        else:
            acc[:, 0:32] += up
            acc[:, 32:64] += down
            bacc[...] += biases
        part[j : j + n] = nn(pre_grad, wu[...]).astype(BF16).reshape(n, 8, 16, 1024)

    own(0)
    own(1)
    own(2)
    second(0)
    own(3)
    wu[0:256] = wu_in[...].T
    for w in weights:
        go(w)
    second(1)
    second(2)
    third(0)
    own(4)
    second(3)
    third(2)
    for w in weights:
        w.wait_recv()
    compute(0, 2)
    own(5)
    second(4)
    third(3)
    own(6)
    second(5)
    compute(2, 2)
    second(6)
    own(7)
    third(5)
    third(6)
    compute(4, 2)
    compute(6, 1)
    compute(7, 1)

    def across(r):
        return remote(cs.at[r], cr.at[r], cs_s.at[r], cs_r.at[r], sibling)

    for r in (8, 7, 9, 5, 11, 6, 10, 3, 13, 4, 12, 1, 15, 2, 14, 0):
        o = lax.rem(z + r, NZ)
        cs[r] = acc[1, pl.ds(o * SUBS, SUBS)].astype(BF16)
        go(across(r))

    right, left = xpeer(1, 0), xpeer(NX - 1, 0)
    lo, hi = pl.ds(0, 4), pl.ds(4, 4)

    def raw_plus():
        return remote(part.at[hi, 2:4], near_r.at[0, hi], p_s.at[2], p_r.at[2], right)

    def raw_minus():
        return remote(part.at[lo, 6:8], near_r.at[1, lo], p_s.at[3], p_r.at[3], left)

    def far_plus():
        return remote(part.at[lo, 4:6], fars.at[0], p_s.at[0], p_r.at[0], right)

    def far_minus():
        return remote(part.at[hi, 4:6], fars.at[1], p_s.at[1], p_r.at[1], left)

    def sum_plus():
        return remote(near_s.at[0], near_r.at[0, lo], p_s.at[4], p_r.at[4], right)

    def sum_minus():
        return remote(near_s.at[1], near_r.at[1, hi], p_s.at[5], p_r.at[5], left)

    def last_leg():
        return remote(ysend, yrecv, p_s.at[6], p_r.at[6], xpeer(0, 1))

    for copy in (far_plus(), far_minus(), raw_plus(), raw_minus()):
        go(copy)

    def along_plus():
        far_plus().wait_recv()
        near_s[0] = (part[0:4, 2:4].astype(F32) + fars[0].astype(F32)).astype(BF16)
        go(sum_plus())

    def along_minus():
        far_minus().wait_recv()
        near_s[1] = (part[4:8, 6:8].astype(F32) + fars[1].astype(F32)).astype(BF16)
        go(sum_minus())

    def across_y():
        for copy in (raw_plus(), raw_minus(), sum_plus(), sum_minus()):
            copy.wait_recv()
        ysend[...] = (
            part[:, 1].astype(F32) + near_r[0, :, 1].astype(F32) + near_r[1, :, 1].astype(F32)
        ).astype(BF16)
        go(last_leg())

    def mine(r, h):
        return acc[0, SUBS * lax.rem(z + r, NZ) + h] + cr[r, h].astype(F32)

    ways = (0, 1)

    def toward(way, d):
        return d if way == 0 else NZ - d

    def feed(way, d):
        return remote(
            fs.at[way, d // 2], fr.at[way, d // 2], fd_s.at[way, d // 2], fd_r.at[way, d // 2],
            zpeer(toward(way, 1), 0),
        )

    def chain(way, d, h):
        i = d // 2 - 1
        return remote(
            sp.at[way, i, h], rp.at[way, i, h], rp_s.at[way, i, h], rp_r.at[way, i, h],
            zpeer(toward(way, 2), 0),
        )

    def feeders(d):
        for way in ways:
            r = toward(way, d)
            across(r).wait_recv()
            for h in range(SUBS):
                fs[way, d // 2, h] = mine(r, h).astype(BF16)
            go(feed(way, d))

    def links(d):
        for way in ways:
            if d == 8 and way:
                continue
            across(toward(way, d)).wait_recv()
            if d < 8:
                feed(way, d + 1).wait_recv()
        for h in range(SUBS):
            for way in ways:
                if d == 8 and way:
                    continue
                value = mine(toward(way, d), h)
                if d < 8:
                    value = value + fr[way, d // 2, h].astype(F32)
                if d < (8 if way == 0 else 6):
                    chain(way, d + 2, h).wait_recv()
                    value = value + rp[way, d // 2, h].astype(F32)
                sp[way, d // 2 - 1, h] = value.astype(BF16)
                go(chain(way, d, h))

    links(8)
    feeders(7)
    feeders(5)
    weighted = jnp.zeros((1, 1024), F32)
    for half in range(2):
        prod = acc[half, 0:32].reshape(256, 1024) * wu[256 * half : 256 * half + 256].astype(F32)
        weighted = weighted + jnp.sum(prod, axis=0, keepdims=True)
    weighted = weighted / gain[...]
    small_s[:, 0:1024] = weighted
    small_s[:, 1024:1280] = bacc[:, 256:512]
    to_sibling = go(remote(small_s, small_r, sm_s.at[0], sm_r.at[0], sibling))
    links(6)
    feeders(3)
    to_sibling.wait_recv()
    whole_gain = weighted + small_r[:, 0:1024]
    for j in range(8):
        gs[j] = whole_gain[:, 128 * j : 128 * j + 128]
    bs[:, 128:384] = bacc[:, 0:256] + small_r[:, 1024:1280]
    here = x * 2 + yh

    def there_of(m):
        return lax.rem(x + m // 2, NX) * 2 + (yh + m % 2) % 2

    ar[here] = gs[here]
    for m in range(1, 8):
        go(
            remote(
                gs.at[there_of(m)], ar.at[here], ga_s.at[m], ga_r.at[here], xpeer(m // 2, m % 2)
            )
        )
    links(4)
    feeders(1)
    along_plus()
    along_minus()
    for m in range(1, 8):
        j = there_of(m)
        remote(gs.at[j], ar.at[j], ga_s.at[m], ga_r.at[j], sibling).wait_recv()
    bs[:, 0:128] = jnp.sum(ar[...], axis=0)
    number = z * 2 + yl
    br[number] = bs[...]
    for t in range(1, 32):
        go(
            remote(
                bs, br.at[number], gb_s.at[t], gb_r.at[number], zpeer(OFFSETS[t // 2], t % 2)
            )
        )
    links(2)

    def swap(h):
        return remote(ys.at[h], yr.at[h], y_s.at[h], y_r.at[h], zpeer(0, 1))

    across(0).wait_recv()
    for way in ways:
        feed(way, 1).wait_recv()
    for h in range(SUBS):
        total = mine(0, h)
        for way in ways:
            chain(way, 2, h).wait_recv()
            total = total + rp[way, 0, h].astype(F32) + fr[way, 0, h].astype(F32)
        ys[h] = total.astype(BF16)
        go(swap(h))

    def spots(way, d, h, n):
        origin = lax.rem(z + toward(1 - way, d), NZ)
        return ag.at[pl.ds(SUBS * origin + h, n)]

    def stride(way, d, h, at):
        spot = spots(way, at, h, 1)
        i = d // 2 - 1
        return remote(
            spot, spot, ap_s.at[way, i, h], ap_r.at[way, i, h], zpeer(toward(way, 2), 0)
        )

    def single(way, d, at):
        spot = spots(way, at, 0, SUBS)
        i = d // 2
        return remote(spot, spot, am_s.at[way, i], am_r.at[way, i], zpeer(toward(way, 1), 0))

    for h in range(SUBS):
        swap(h).wait_recv()
        ag[SUBS * z + h] = (ys[h].astype(F32) + yr[h].astype(F32)).astype(BF16)
        for way in ways:
            go(stride(way, 2, h, 0))
    for way in ways:
        go(single(way, 1, 0))
    across_y()

    def turn(d):
        for h in range(SUBS):
            for way in ways:
                stride(way, d, h, d).wait_recv()
                if d < (8 if way == 0 else 6):
                    go(stride(way, d + 2, h, d))
        for way in ways:
            go(single(way, d + 1, d))

    for t in range(1, 32):
        source = lax.rem(z + OFFSETS[t // 2], NZ) * 2 + (yl + t % 2) % 2
        remote(bs, br.at[source], gb_s.at[t], gb_r.at[source], sibling).wait_recv()
    sums = jnp.sum(br[...], axis=0)
    bias_out[...] = sums[:, 128:384]
    cc_s[...] = sums[:, 0:128]
    cr_r[here] = sums[:, 0:128]
    for m in range(1, 8):
        go(remote(cc_s, cr_r.at[here], gc_s.at[m], gc_r.at[here], xpeer(m // 2, m % 2)))
    turn(2)
    turn(4)
    turn(6)

    last_leg().wait_recv()
    for i in range(4):
        k = pl.ds(2 * i, 2)
        summed = (
            part[k, 0].astype(F32)
            + near_r[0, k, 0].astype(F32)
            + near_r[1, k, 0].astype(F32)
            + yrecv[k].astype(F32)
        ).reshape(32, 1024)
        scaled = summed * gain[...]
        standard = xh[k].reshape(32, 1024)
        first = jnp.mean(scaled, axis=1, keepdims=True)
        cross = jnp.mean(scaled * standard, axis=1, keepdims=True)
        inverse = rs[k].reshape(32, 128)[:, 0:1]
        value = g[k, 1, 0].reshape(32, 1024).astype(F32) + inverse * (
            scaled - first - standard * cross
        )
        dxs[k] = value.astype(BF16).reshape(2, 16, 1024)
    for way in ways:
        for d in (1, 3, 5, 7):
            single(way, d, d).wait_recv()
    for h in range(SUBS):
        stride(0, 8, h, 8).wait_recv()
    ag_out[...] = ag[...]
    for m in range(1, 8):
        j = there_of(m)
        remote(cc_s, cr_r.at[j], gc_s.at[m], gc_r.at[j], sibling).wait_recv()
    gain_out[...] = cr_r[...].reshape(8, 128)
    for copy in pending:
        copy.wait_send()


def finish(dxs, up, down, bias, gain, dx_out, up_out, down_out, bias_out, gain_out):
    z, yl = lax.axis_index("dp_0"), lax.axis_index("dp_1")
    spot = iota((64, 128), 1)
    tile = spot // 4
    at = tile // 2
    offset = jnp.where(at == 0, 0, jnp.where(at % 2 == 1, (at + 1) // 2, NZ - at // 2))
    source = ((z - offset + NZ) & (NZ - 1)) * 2 + (((tile % 2) + yl) & 1)
    row = iota((64, 128), 0) + 64 * pl.program_id(0)
    perm = (row == source * 4 + spot % 4).astype(BF16)
    dx_out[...] = nn(perm, dxs[...].reshape(128, 1024)).astype(BF16)
    up_out[...] = up[...].reshape(128, 1024).astype(F32).T
    down_out[...] = down[...].reshape(128, 1024).astype(F32)
    bias_out[...] = bias[...]
    gain_out[...] = gain[...]


def shards(tokens, cotangent, routes, norm_gain_vector, up_weight, up_bias, down_weight):
    vmem, sem = pltpu.VMEM, pltpu.SemaphoreType.DMA
    dxs, sums, bias, gain = pl.pallas_call(
        kernel,
        out_shape=(
            jax.ShapeDtypeStruct((CHUNKS, 16, 1024), BF16),
            jax.ShapeDtypeStruct((64, 8, 1024), BF16),
            jax.ShapeDtypeStruct((1, 256), F32),
            jax.ShapeDtypeStruct((8, 128), F32),
        ),
        in_specs=[pl.BlockSpec(memory_space=pltpu.VMEM)] * 7,
        out_specs=[pl.BlockSpec(memory_space=pltpu.VMEM)] * 4,
        scratch_shapes=[
            vmem((32, 8, 1024), BF16),
            vmem((32, 8, 1024), BF16),
            vmem((CHUNKS, 2, 8, 16, 1024), BF16),
            vmem((512, 1024), BF16),
            vmem((512, 1024), BF16),
            vmem((2, 1, 256), F32),
            vmem((2, 64, 8, 1024), F32),
            vmem((1, 512), F32),
            vmem((CHUNKS, 8, 16, 1024), BF16),
            vmem((2, 4, 2, 16, 1024), BF16),
            vmem((2, 4, 2, 16, 1024), BF16),
            vmem((2, CHUNKS, 2, 16, 1024), BF16),
            vmem((CHUNKS, 16, 1024), BF16),
            vmem((CHUNKS, 16, 1024), BF16),
            vmem((CHUNKS, 16, 1024), F32),
            vmem((CHUNKS, 16, 128), F32),
            vmem((16, SUBS, 8, 1024), BF16),
            vmem((16, SUBS, 8, 1024), BF16),
            vmem((2, 4, SUBS, 8, 1024), BF16),
            vmem((2, 4, SUBS, 8, 1024), BF16),
            vmem((2, 4, SUBS, 8, 1024), BF16),
            vmem((2, 4, SUBS, 8, 1024), BF16),
            vmem((SUBS, 8, 1024), BF16),
            vmem((SUBS, 8, 1024), BF16),
            vmem((64, 8, 1024), BF16),
            vmem((1, 1280), F32),
            vmem((1, 1280), F32),
            vmem((8, 1, 128), F32),
            vmem((8, 1, 128), F32),
            vmem((1, 384), F32),
            vmem((32, 1, 384), F32),
            vmem((1, 128), F32),
            vmem((8, 1, 128), F32),
            sem((32,)), sem((32,)),
            sem((CHUNKS, 8)), sem((CHUNKS, 8)),
            sem((3,)), sem((3,)),
            sem((8,)), sem((8,)),
            sem((16,)), sem((16,)),
            sem((2, 4)), sem((2, 4)),
            sem((2, 4, SUBS)), sem((2, 4, SUBS)),
            sem((SUBS,)), sem((SUBS,)),
            sem((2, 4, SUBS)), sem((2, 4, SUBS)),
            sem((2, 4)), sem((2, 4)),
            sem((1,)), sem((1,)),
            sem((8,)), sem((8,)),
            sem((32,)), sem((32,)),
            sem((8,)), sem((8,)),
        ],
        compiler_params=pltpu.CompilerParams(
            collective_id=0, has_side_effects=True, vmem_limit_bytes=60 * 1024 * 1024
        ),
        name="ffn_backward",
    )(
        tokens,
        cotangent,
        routes.reshape(1, -1),
        norm_gain_vector.reshape(1, -1),
        up_weight,
        up_bias.reshape(1, -1),
        down_weight,
    )
    dx, up, down, bias, gain = pl.pallas_call(
        finish,
        grid=(2,),
        out_shape=(
            jax.ShapeDtypeStruct((128, 1024), BF16),
            jax.ShapeDtypeStruct((1024, 256), F32),
            jax.ShapeDtypeStruct((256, 1024), F32),
            jax.ShapeDtypeStruct((1, 256), F32),
            jax.ShapeDtypeStruct((8, 128), F32),
        ),
        in_specs=[
            pl.BlockSpec((CHUNKS, 16, 1024), lambda i: (0, 0, 0)),
            pl.BlockSpec((16, 8, 1024), lambda i: (i, 0, 0)),
            pl.BlockSpec((16, 8, 1024), lambda i: (2 + i, 0, 0)),
            pl.BlockSpec((1, 256), lambda i: (0, 0)),
            pl.BlockSpec((8, 128), lambda i: (0, 0)),
        ],
        out_specs=[
            pl.BlockSpec((64, 1024), lambda i: (i, 0)),
            pl.BlockSpec((1024, 128), lambda i: (0, i)),
            pl.BlockSpec((128, 1024), lambda i: (i, 0)),
            pl.BlockSpec((1, 256), lambda i: (0, 0)),
            pl.BlockSpec((8, 128), lambda i: (0, 0)),
        ],
        name="finish",
    )(dxs, sums, sums, bias, gain)
    return (dx, up, bias.reshape(-1), down, gain.reshape(-1))


def solution(mesh):
    finer = Mesh(mesh.devices.reshape(NZ, 2, NX, 2, 2), DP_FSDP)
    return jax.shard_map(
        shards,
        mesh=finer,
        in_specs=(
            P(DP_FSDP, None),
            P(DP_FSDP, None),
            P(DP_FSDP, None),
            P(),
            P(None, FSDP),
            P(FSDP),
            P(FSDP, None),
        ),
        out_specs=(P(DP_FSDP, None), P(None, FSDP), P(FSDP), P(FSDP, None), P()),
        check_vma=False,
    )
```

```python
import jax
import jax.numpy as jnp
from jax import lax
from jax.experimental import pallas as pl
from jax.experimental.pallas import tpu as pltpu
from jax.sharding import Mesh
from jax.sharding import PartitionSpec as P

FSDP = ("fsdp_0", "fsdp_1", "fsdp_2")
DP_FSDP = ("dp_0", "dp_1", "fsdp_0", "fsdp_1", "fsdp_2")
MESH = pl.DeviceIdType.MESH

root_two_pi = 0.7978845608
cubic = 0.044715

NZ, NX = 16, 4
OFFSETS = [0, 1, 15, 2, 14, 3, 13, 4, 12, 5, 11, 6, 10, 7, 9, 8]
CHUNKS, SUBS = 8, 4
F32, BF16 = jnp.float32, jnp.bfloat16


def gelu_pair(pre):
    inner = root_two_pi * (pre + cubic * pre * pre * pre)
    tangent = jnp.tanh(inner)
    act = 0.5 * pre * (1.0 + tangent)
    slope = 0.5 * (1.0 + tangent) + 0.5 * pre * (1.0 - tangent * tangent) * root_two_pi * (
        1.0 + 3.0 * cubic * pre * pre
    )
    return (act, slope)


def nn(a, b):
    return lax.dot_general(a, b, (((1,), (0,)), ((), ())), preferred_element_type=F32)


def nt(a, b):
    return lax.dot_general(a, b, (((1,), (1,)), ((), ())), preferred_element_type=F32)


def tn(a, b):
    return lax.dot_general(a, b, (((0,), (0,)), ((), ())), preferred_element_type=F32)


def iota(shape, dim):
    return lax.broadcasted_iota(jnp.int32, shape, dim)


def kernel(
    tok, cot, routes, gain, wu_in, bu_in, wd_in,
    dxs, ag_out, bias_out, gain_out,
    send, land, g, wu, wd, bu, acc, bacc, part, fars, near_s, near_r, ysend, yrecv, xh, rs,
    cs, cr, fs, fr, sp, rp, ys, yr, ag,
    small_s, small_r, gs, ar, bs, br, cc_s, cr_r,
    a2a_s, a2a_r, gat_s, gat_r, hf_s, hf_r, w_s, w_r, p_s, p_r, cs_s, cs_r,
    fd_s, fd_r, rp_s, rp_r, y_s, y_r, ap_s, ap_r, am_s, am_r,
    sm_s, sm_r, ga_s, ga_r, gb_s, gb_r, gc_s, gc_r,
):
    z, yl = lax.axis_index("dp_0"), lax.axis_index("dp_1")
    x, yh, c = lax.axis_index("fsdp_0"), lax.axis_index("fsdp_1"), lax.axis_index("fsdp_2")
    pending = []

    def zpeer(dz, dy):
        return (lax.rem(z + dz, NZ), (yl + dy) % 2, x, yh, c)

    def xpeer(rx, ry):
        return (z, yl, lax.rem(x + rx, NX), (yh + ry) % 2, c)

    sibling = (z, yl, x, yh, 1 - c)

    def remote(src, dst, ssem, rsem, peer):
        return pltpu.make_async_remote_copy(
            src_ref=src, dst_ref=dst, send_sem=ssem, recv_sem=rsem,
            device_id=peer, device_id_type=MESH,
        )

    def go(copy):
        copy.start()
        pending.append(copy)
        return copy

    barrier = pltpu.get_barrier_semaphore()
    peers = [zpeer(dz, dy) for dz in range(NZ) for dy in range(2) if dz or dy]
    peers += [xpeer(rx, ry) for rx in range(NX) for ry in range(2) if rx or ry]
    peers.append(sibling)
    for peer in peers:
        pl.semaphore_signal(barrier, inc=1, device_id=peer, device_id_type=MESH)

    target = routes[...]
    hot = (iota((40, 128), 0) == target).astype(BF16)
    before = (iota((128, 128), 0) < iota((128, 128), 1)).astype(BF16)
    ranked = jnp.sum(nn(hot, before) * hot.astype(F32), axis=0, keepdims=True).astype(jnp.int32)
    dz = ((target >> 1) - z + NZ) & (NZ - 1)
    pos = jnp.where(dz == 0, 0, jnp.where(dz <= NZ // 2, 2 * dz - 1, 2 * (NZ - dz)))
    dy = ((target & 1) + yl) & 1
    row = jnp.where(target < 2 * NZ, (pos * 2 + dy) * 8 + ranked, -8)
    line = iota((256, 128), 0)
    placed = nn((line == row).astype(BF16), tok[...]) + nn(
        (line == row + 4).astype(BF16), cot[...]
    )
    send[...] = placed.astype(BF16).reshape(32, 8, 1024)
    land[0] = send[0]

    pl.semaphore_wait(barrier, len(peers))

    a2a = {}
    for t in range(1, 32):
        a2a[t] = go(
            remote(send.at[t], land.at[t], a2a_s.at[t], a2a_r.at[t], zpeer(OFFSETS[t // 2], t % 2))
        )
    weights = [
        (remote(wu.at[0:256], wu.at[256:512], w_s.at[0], w_r.at[0], sibling)),
        (remote(wd_in, wd.at[256:512], w_s.at[1], w_r.at[1], sibling)),
        (remote(bu_in, bu.at[1], w_s.at[2], w_r.at[2], sibling)),
    ]

    STAGED_Y, STAGED_X, DIRECT = 0, 1, 2
    plan = [STAGED_Y, STAGED_X, STAGED_Y, STAGED_Y, STAGED_X, STAGED_Y, STAGED_Y, DIRECT]
    here_now = set()

    def push(k, src, dst, rx, ry):
        go(
            remote(
                g.at[k, :, src], g.at[k, :, dst], gat_s.at[k, dst], gat_r.at[k, dst], xpeer(rx, ry)
            )
        )

    def half(h, src, dst, peer):
        rows = pl.ds(8 * h, 8)
        return remote(
            g.at[CHUNKS - 1, :, src, rows], g.at[CHUNKS - 1, :, dst, rows],
            hf_s.at[h, dst], hf_r.at[h, dst], peer,
        )

    def need(k, slot):
        if (k, slot) not in here_now:
            here_now.add((k, slot))
            if plan[k] == DIRECT:
                for h in range(2):
                    half(h, slot, slot, sibling).wait_recv()
            else:
                spot = g.at[k, :, slot]
                remote(spot, spot, gat_s.at[k, slot], gat_r.at[k, slot], sibling).wait_recv()

    sorter = iota((32, 32), 0)
    column = iota((32, 32), 1)
    wanted = (column // 8) * 4 + (column % 4) + jnp.where(column % 8 >= 4, 16, 0)
    sort = (sorter == wanted).astype(BF16)

    def own(k):
        for t in range(4 * k, 4 * k + 4):
            if t:
                a2a[t].wait_recv()
        rows = nn(sort, land[4 * k : 4 * k + 4].reshape(32, 1024))
        values = rows[0:16]
        centered = values - jnp.mean(values, axis=1, keepdims=True)
        variance = jnp.mean(centered * centered, axis=1, keepdims=True)
        inverse = 1.0 / jnp.sqrt(variance + 1e-05)
        standard = centered * inverse
        xh[k] = standard
        rs[k] = jnp.broadcast_to(inverse, (16, 128))
        g[k, 0, 0] = (standard * gain[...]).astype(BF16)
        g[k, 1, 0] = rows[16:32].astype(BF16)
        if plan[k] == STAGED_Y:
            push(k, 0, 1, 0, 1)
            push(k, 0, 6, 1, 0)
            push(k, 0, 2, 3, 0)
        elif plan[k] == STAGED_X:
            push(k, 0, 4, 2, 0)
            push(k, 0, 6, 1, 0)
            push(k, 0, 2, 3, 0)
            push(k, 0, 1, 0, 1)

    def own_half(h):
        k, at = CHUNKS - 1, 4 * (CHUNKS - 1) + 2 * h
        for t in (at, at + 1):
            a2a[t].wait_recv()
        order = iota((16, 16), 1)
        goal = (order // 8) * 4 + (order % 4) + jnp.where(order % 8 >= 4, 8, 0)
        rows = nn((iota((16, 16), 0) == goal).astype(BF16), land[at : at + 2].reshape(16, 1024))
        values = rows[0:8]
        centered = values - jnp.mean(values, axis=1, keepdims=True)
        variance = jnp.mean(centered * centered, axis=1, keepdims=True)
        inverse = 1.0 / jnp.sqrt(variance + 1e-05)
        standard = centered * inverse
        spot = slice(8 * h, 8 * h + 8)
        xh[k, spot] = standard
        rs[k, spot] = jnp.broadcast_to(inverse, (8, 128))
        g[k, 0, 0, spot] = (standard * gain[...]).astype(BF16)
        g[k, 1, 0, spot] = rows[8:16].astype(BF16)
        for rx, ry in ((2, 1), (1, 1), (3, 1), (0, 1), (2, 0), (1, 0), (3, 0)):
            go(half(h, 0, ((NX - rx) % NX) * 2 + ry, xpeer(rx, ry)))

    def second(k):
        if plan[k] == STAGED_Y:
            need(k, 1)
            push(k, 1, 7, 1, 0)
            push(k, 1, 3, 3, 0)
        else:
            for slot in (6, 2, 4):
                need(k, slot)
                push(k, slot, slot + 1, 0, 1)

    def third(k):
        need(k, 6)
        push(k, 6, 4, 1, 0)
        need(k, 3)
        push(k, 3, 5, 3, 0)

    def compute(j, n):
        for k in range(j, j + n):
            for slot in range(1, 8):
                need(k, slot)
        normed = g[j : j + n, 0].reshape(128 * n, 1024)
        outer = g[j : j + n, 1].reshape(128 * n, 1024)
        bias = jnp.concatenate([bu[0], bu[1]], axis=1)
        act, slope = gelu_pair(nt(normed, wu[...]) + bias)
        pre_grad = (nt(outer, wd[...]) * slope).astype(BF16)
        act = act.astype(BF16)
        up = tn(pre_grad, normed).reshape(2, 32, 8, 1024)
        down = tn(act, outer).reshape(2, 32, 8, 1024)
        biases = jnp.sum(pre_grad.astype(F32), axis=0, keepdims=True)
        if j == 0:
            acc[:, 0:32] = up
            acc[:, 32:64] = down
            bacc[...] = biases
        else:
            acc[:, 0:32] += up
            acc[:, 32:64] += down
            bacc[...] += biases
        part[j : j + n] = nn(pre_grad, wu[...]).astype(BF16).reshape(n, 8, 16, 1024)

    own(0)
    own(1)
    own(2)
    second(0)
    own(3)
    wd[0:256] = wd_in[...]
    bu[0] = bu_in[...]
    wu[0:256] = wu_in[...].T
    for w in weights:
        go(w)
    second(1)
    second(2)
    third(0)
    own(4)
    second(3)
    third(2)
    for w in weights:
        w.wait_recv()
    compute(0, 2)
    own(5)
    second(4)
    third(3)
    own(6)
    second(5)
    compute(2, 2)
    own_half(0)
    second(6)
    own_half(1)
    third(5)
    third(6)
    compute(4, 2)
    compute(6, 1)
    compute(7, 1)

    def across(r):
        return remote(cs.at[r], cr.at[r], cs_s.at[r], cs_r.at[r], sibling)

    for r in (8, 7, 9, 5, 11, 6, 10, 3, 13, 4, 12, 1, 15, 2, 14, 0):
        o = lax.rem(z + r, NZ)
        cs[r] = acc[1, pl.ds(o * SUBS, SUBS)].astype(BF16)
        go(across(r))

    right, left = xpeer(1, 0), xpeer(NX - 1, 0)
    lo, hi = pl.ds(0, 4), pl.ds(4, 4)

    def raw_plus():
        return remote(part.at[hi, 2:4], near_r.at[0, hi], p_s.at[2], p_r.at[2], right)

    def raw_minus():
        return remote(part.at[lo, 6:8], near_r.at[1, lo], p_s.at[3], p_r.at[3], left)

    def far_plus():
        return remote(part.at[lo, 4:6], fars.at[0], p_s.at[0], p_r.at[0], right)

    def far_minus():
        return remote(part.at[hi, 4:6], fars.at[1], p_s.at[1], p_r.at[1], left)

    def sum_plus():
        return remote(near_s.at[0], near_r.at[0, lo], p_s.at[4], p_r.at[4], right)

    def sum_minus():
        return remote(near_s.at[1], near_r.at[1, hi], p_s.at[5], p_r.at[5], left)

    def last_leg():
        return remote(ysend, yrecv, p_s.at[6], p_r.at[6], xpeer(0, 1))

    for copy in (far_plus(), far_minus(), raw_plus(), raw_minus()):
        go(copy)

    def along_plus():
        far_plus().wait_recv()
        near_s[0] = (part[0:4, 2:4].astype(F32) + fars[0].astype(F32)).astype(BF16)
        go(sum_plus())

    def along_minus():
        far_minus().wait_recv()
        near_s[1] = (part[4:8, 6:8].astype(F32) + fars[1].astype(F32)).astype(BF16)
        go(sum_minus())

    def across_y():
        for copy in (raw_plus(), raw_minus(), sum_plus(), sum_minus()):
            copy.wait_recv()
        ysend[...] = (
            part[:, 1].astype(F32) + near_r[0, :, 1].astype(F32) + near_r[1, :, 1].astype(F32)
        ).astype(BF16)
        go(last_leg())

    def mine(r, h):
        return acc[0, SUBS * lax.rem(z + r, NZ) + h] + cr[r, h].astype(F32)

    ways = (0, 1)

    def toward(way, d):
        return d if way == 0 else NZ - d

    def feed(way, d):
        return remote(
            fs.at[way, d // 2], fr.at[way, d // 2], fd_s.at[way, d // 2], fd_r.at[way, d // 2],
            zpeer(toward(way, 1), 0),
        )

    def chain(way, d, h):
        i = d // 2 - 1
        return remote(
            sp.at[way, i, h], rp.at[way, i, h], rp_s.at[way, i, h], rp_r.at[way, i, h],
            zpeer(toward(way, 2), 0),
        )

    def feeders(d):
        for way in ways:
            r = toward(way, d)
            across(r).wait_recv()
            for h in range(SUBS):
                fs[way, d // 2, h] = mine(r, h).astype(BF16)
            go(feed(way, d))

    def links(d):
        for way in ways:
            if d == 8 and way:
                continue
            across(toward(way, d)).wait_recv()
            if d < 8:
                feed(way, d + 1).wait_recv()
        for h in range(SUBS):
            for way in ways:
                if d == 8 and way:
                    continue
                value = mine(toward(way, d), h)
                if d < 8:
                    value = value + fr[way, d // 2, h].astype(F32)
                if d < (8 if way == 0 else 6):
                    chain(way, d + 2, h).wait_recv()
                    value = value + rp[way, d // 2, h].astype(F32)
                sp[way, d // 2 - 1, h] = value.astype(BF16)
                go(chain(way, d, h))

    links(8)
    feeders(7)
    feeders(5)
    weighted = jnp.zeros((1, 1024), F32)
    for half in range(2):
        prod = acc[half, 0:32].reshape(256, 1024) * wu[256 * half : 256 * half + 256].astype(F32)
        weighted = weighted + jnp.sum(prod, axis=0, keepdims=True)
    weighted = weighted / gain[...]
    small_s[:, 0:1024] = weighted
    small_s[:, 1024:1280] = bacc[:, 256:512]
    to_sibling = go(remote(small_s, small_r, sm_s.at[0], sm_r.at[0], sibling))
    links(6)
    feeders(3)
    to_sibling.wait_recv()
    whole_gain = weighted + small_r[:, 0:1024]
    for j in range(8):
        gs[j] = whole_gain[:, 128 * j : 128 * j + 128]
    bs[:, 128:384] = bacc[:, 0:256] + small_r[:, 1024:1280]
    here = x * 2 + yh

    def there_of(m):
        return lax.rem(x + m // 2, NX) * 2 + (yh + m % 2) % 2

    ar[here] = gs[here]
    for m in range(1, 8):
        go(
            remote(
                gs.at[there_of(m)], ar.at[here], ga_s.at[m], ga_r.at[here], xpeer(m // 2, m % 2)
            )
        )
    links(4)
    feeders(1)
    along_plus()
    along_minus()
    for m in range(1, 8):
        j = there_of(m)
        remote(gs.at[j], ar.at[j], ga_s.at[m], ga_r.at[j], sibling).wait_recv()
    bs[:, 0:128] = jnp.sum(ar[...], axis=0)
    number = z * 2 + yl
    br[number] = bs[...]
    for t in range(1, 32):
        go(
            remote(
                bs, br.at[number], gb_s.at[t], gb_r.at[number], zpeer(OFFSETS[t // 2], t % 2)
            )
        )
    links(2)

    def swap(h):
        return remote(ys.at[h], yr.at[h], y_s.at[h], y_r.at[h], zpeer(0, 1))

    across(0).wait_recv()
    for way in ways:
        feed(way, 1).wait_recv()
    for h in range(SUBS):
        total = mine(0, h)
        for way in ways:
            chain(way, 2, h).wait_recv()
            total = total + rp[way, 0, h].astype(F32) + fr[way, 0, h].astype(F32)
        ys[h] = total.astype(BF16)
        go(swap(h))

    def spots(way, d, h, n):
        origin = lax.rem(z + toward(1 - way, d), NZ)
        return ag.at[pl.ds(SUBS * origin + h, n)]

    def stride(way, d, h, at):
        spot = spots(way, at, h, 1)
        i = d // 2 - 1
        return remote(
            spot, spot, ap_s.at[way, i, h], ap_r.at[way, i, h], zpeer(toward(way, 2), 0)
        )

    def single(way, d, at):
        spot = spots(way, at, 0, SUBS)
        i = d // 2
        return remote(spot, spot, am_s.at[way, i], am_r.at[way, i], zpeer(toward(way, 1), 0))

    for h in range(SUBS):
        swap(h).wait_recv()
        ag[SUBS * z + h] = (ys[h].astype(F32) + yr[h].astype(F32)).astype(BF16)
        for way in ways:
            go(stride(way, 2, h, 0))
    for way in ways:
        go(single(way, 1, 0))
    across_y()

    def turn(d):
        for h in range(SUBS):
            for way in ways:
                stride(way, d, h, d).wait_recv()
                if d < (8 if way == 0 else 6):
                    go(stride(way, d + 2, h, d))
        for way in ways:
            go(single(way, d + 1, d))

    for t in range(1, 32):
        source = lax.rem(z + OFFSETS[t // 2], NZ) * 2 + (yl + t % 2) % 2
        remote(bs, br.at[source], gb_s.at[t], gb_r.at[source], sibling).wait_recv()
    sums = jnp.sum(br[...], axis=0)
    bias_out[...] = sums[:, 128:384]
    cc_s[...] = sums[:, 0:128]
    cr_r[here] = sums[:, 0:128]
    for m in range(1, 8):
        go(remote(cc_s, cr_r.at[here], gc_s.at[m], gc_r.at[here], xpeer(m // 2, m % 2)))
    turn(2)
    turn(4)
    turn(6)

    last_leg().wait_recv()
    for i in range(4):
        k = pl.ds(2 * i, 2)
        summed = (
            part[k, 0].astype(F32)
            + near_r[0, k, 0].astype(F32)
            + near_r[1, k, 0].astype(F32)
            + yrecv[k].astype(F32)
        ).reshape(32, 1024)
        scaled = summed * gain[...]
        standard = xh[k].reshape(32, 1024)
        first = jnp.mean(scaled, axis=1, keepdims=True)
        cross = jnp.mean(scaled * standard, axis=1, keepdims=True)
        inverse = rs[k].reshape(32, 128)[:, 0:1]
        value = g[k, 1, 0].reshape(32, 1024).astype(F32) + inverse * (
            scaled - first - standard * cross
        )
        dxs[k] = value.astype(BF16).reshape(2, 16, 1024)
    for way in ways:
        for d in (1, 3, 5, 7):
            single(way, d, d).wait_recv()
    for h in range(SUBS):
        stride(0, 8, h, 8).wait_recv()
    ag_out[...] = ag[...]
    for m in range(1, 8):
        j = there_of(m)
        remote(cc_s, cr_r.at[j], gc_s.at[m], gc_r.at[j], sibling).wait_recv()
    gain_out[...] = cr_r[...].reshape(8, 128)
    for copy in pending:
        copy.wait_send()


def finish(dxs, up, down, bias, gain, dx_out, up_out, down_out, bias_out, gain_out):
    z, yl = lax.axis_index("dp_0"), lax.axis_index("dp_1")
    spot = iota((64, 128), 1)
    tile = spot // 4
    at = tile // 2
    offset = jnp.where(at == 0, 0, jnp.where(at % 2 == 1, (at + 1) // 2, NZ - at // 2))
    source = ((z - offset + NZ) & (NZ - 1)) * 2 + (((tile % 2) + yl) & 1)
    row = iota((64, 128), 0) + 64 * pl.program_id(0)
    perm = (row == source * 4 + spot % 4).astype(BF16)
    dx_out[...] = nn(perm, dxs[...].reshape(128, 1024)).astype(BF16)
    up_out[...] = up[...].reshape(128, 1024).astype(F32).T
    down_out[...] = down[...].reshape(128, 1024).astype(F32)
    bias_out[...] = bias[...]
    gain_out[...] = gain[...]


def shards(tokens, cotangent, routes, norm_gain_vector, up_weight, up_bias, down_weight):
    vmem, sem = pltpu.VMEM, pltpu.SemaphoreType.DMA
    dxs, sums, bias, gain = pl.pallas_call(
        kernel,
        out_shape=(
            jax.ShapeDtypeStruct((CHUNKS, 16, 1024), BF16),
            jax.ShapeDtypeStruct((64, 8, 1024), BF16),
            jax.ShapeDtypeStruct((1, 256), F32),
            jax.ShapeDtypeStruct((8, 128), F32),
        ),
        in_specs=[pl.BlockSpec(memory_space=pltpu.VMEM)] * 7,
        out_specs=[pl.BlockSpec(memory_space=pltpu.VMEM)] * 4,
        scratch_shapes=[
            vmem((32, 8, 1024), BF16),
            vmem((32, 8, 1024), BF16),
            vmem((CHUNKS, 2, 8, 16, 1024), BF16),
            vmem((512, 1024), BF16),
            vmem((512, 1024), BF16),
            vmem((2, 1, 256), F32),
            vmem((2, 64, 8, 1024), F32),
            vmem((1, 512), F32),
            vmem((CHUNKS, 8, 16, 1024), BF16),
            vmem((2, 4, 2, 16, 1024), BF16),
            vmem((2, 4, 2, 16, 1024), BF16),
            vmem((2, CHUNKS, 2, 16, 1024), BF16),
            vmem((CHUNKS, 16, 1024), BF16),
            vmem((CHUNKS, 16, 1024), BF16),
            vmem((CHUNKS, 16, 1024), F32),
            vmem((CHUNKS, 16, 128), F32),
            vmem((16, SUBS, 8, 1024), BF16),
            vmem((16, SUBS, 8, 1024), BF16),
            vmem((2, 4, SUBS, 8, 1024), BF16),
            vmem((2, 4, SUBS, 8, 1024), BF16),
            vmem((2, 4, SUBS, 8, 1024), BF16),
            vmem((2, 4, SUBS, 8, 1024), BF16),
            vmem((SUBS, 8, 1024), BF16),
            vmem((SUBS, 8, 1024), BF16),
            vmem((64, 8, 1024), BF16),
            vmem((1, 1280), F32),
            vmem((1, 1280), F32),
            vmem((8, 1, 128), F32),
            vmem((8, 1, 128), F32),
            vmem((1, 384), F32),
            vmem((32, 1, 384), F32),
            vmem((1, 128), F32),
            vmem((8, 1, 128), F32),
            sem((32,)), sem((32,)),
            sem((CHUNKS, 8)), sem((CHUNKS, 8)),
            sem((2, 8)), sem((2, 8)),
            sem((3,)), sem((3,)),
            sem((8,)), sem((8,)),
            sem((16,)), sem((16,)),
            sem((2, 4)), sem((2, 4)),
            sem((2, 4, SUBS)), sem((2, 4, SUBS)),
            sem((SUBS,)), sem((SUBS,)),
            sem((2, 4, SUBS)), sem((2, 4, SUBS)),
            sem((2, 4)), sem((2, 4)),
            sem((1,)), sem((1,)),
            sem((8,)), sem((8,)),
            sem((32,)), sem((32,)),
            sem((8,)), sem((8,)),
        ],
        compiler_params=pltpu.CompilerParams(
            collective_id=0, has_side_effects=True, vmem_limit_bytes=60 * 1024 * 1024
        ),
        name="ffn_backward",
    )(
        tokens,
        cotangent,
        routes.reshape(1, -1),
        norm_gain_vector.reshape(1, -1),
        up_weight,
        up_bias.reshape(1, -1),
        down_weight,
    )
    dx, up, down, bias, gain = pl.pallas_call(
        finish,
        grid=(2,),
        out_shape=(
            jax.ShapeDtypeStruct((128, 1024), BF16),
            jax.ShapeDtypeStruct((1024, 256), F32),
            jax.ShapeDtypeStruct((256, 1024), F32),
            jax.ShapeDtypeStruct((1, 256), F32),
            jax.ShapeDtypeStruct((8, 128), F32),
        ),
        in_specs=[
            pl.BlockSpec((CHUNKS, 16, 1024), lambda i: (0, 0, 0)),
            pl.BlockSpec((16, 8, 1024), lambda i: (i, 0, 0)),
            pl.BlockSpec((16, 8, 1024), lambda i: (2 + i, 0, 0)),
            pl.BlockSpec((1, 256), lambda i: (0, 0)),
            pl.BlockSpec((8, 128), lambda i: (0, 0)),
        ],
        out_specs=[
            pl.BlockSpec((64, 1024), lambda i: (i, 0)),
            pl.BlockSpec((1024, 128), lambda i: (0, i)),
            pl.BlockSpec((128, 1024), lambda i: (i, 0)),
            pl.BlockSpec((1, 256), lambda i: (0, 0)),
            pl.BlockSpec((8, 128), lambda i: (0, 0)),
        ],
        name="finish",
    )(dxs, sums, sums, bias, gain)
    return (dx, up, bias.reshape(-1), down, gain.reshape(-1))


def solution(mesh):
    finer = Mesh(mesh.devices.reshape(NZ, 2, NX, 2, 2), DP_FSDP)
    return jax.shard_map(
        shards,
        mesh=finer,
        in_specs=(
            P(DP_FSDP, None),
            P(DP_FSDP, None),
            P(DP_FSDP, None),
            P(),
            P(None, FSDP),
            P(FSDP),
            P(FSDP, None),
        ),
        out_specs=(P(DP_FSDP, None), P(None, FSDP), P(FSDP), P(FSDP, None), P()),
        check_vma=False,
    )
```
